512 devices in a mesh: vec: 32 (over y_lo, z), gz: 16 (over x, y_hi, core).
Axes of the slice: x: 4, y: 4 (y_hi: 2, y_lo: 2; y = y_hi * 2 + y_lo), z: 16, core: 2. Of those that a mesh axis runs over, the one named last changes fastest.
Arguments:
- base_flow: float32 [3, 128, 128, 128], P(None, 'gz'), may hold values from -6 to 6
- tangents: float32 [32, 3, 128, 128, 128], P('vec', None, 'gz'), may hold values from -6 to 6
- shells: int32 [4], replicated, may hold values from 1 to 31
Outputs:
- base_next: float32 [3, 128, 128, 128], P(None, 'gz', 'vec')
- ortho_tangents: float32 [32, 3, 128, 128, 128], P('vec', None, 'gz')
- growth: float32 [32], replicated
The draws below stay inside these ranges and needn't reach their ends.
Inputs may be any that keep to these rules, and one draw needn't show every extreme that they name: `shells`: repeats may occur.
All inputs are finite; a program needn't handle non-finite values.
Results may differ from the reference program's by a relative error of at most 0.00017.
Values sent between devices are 32-bit elements; how exact they have to be, the bound alone decides.
A program may use at most 128 MiB of HBM per device.

```python
import math
import jax
import jax.numpy as jnp
from jax import lax

NX = 128
NY = 128
NZ = 128
NFORCE = 4
VECS = 32


def set_ends(array, own_key, least, largest):
    longest = array.shape.index(max(array.shape))
    spots = []
    for shift in (0, 1):
        where = [jax.random.randint(jax.random.fold_in(own_key, axis), (), 0, length) for axis, length in enumerate(array.shape)]
        where[longest] = (where[longest] + shift) % array.shape[longest]
        spots.append(tuple(where))
    return array.at[spots[0]].set(least).at[spots[1]].set(largest)


def steps_of(key, shape, split, smallest, top_value):
    factor_of, own = 1.0, jax.random.fold_in(key, 6)
    for dim, blocks in split:
        draws = jnp.exp(jax.random.uniform(jax.random.fold_in(own, dim), (blocks,), jnp.float32, smallest / len(split), top_value / len(split)))
        factor_of = factor_of * jnp.repeat(draws, shape[dim] // blocks).reshape([-1 if axis == dim else 1 for axis in range(len(shape))])
    return factor_of


def bell_draw(key, shape, width, reach, cuts=(), held_as=jnp.bfloat16):
    entries = jax.random.normal(key, shape, jnp.float32) * width
    if len(cuts) > 0:
        entries = steps_of(key, shape, cuts, -0.22, 0.18) * entries
    return jnp.clip(entries, min=-reach, max=reach).astype(held_as)


def setup_inputs(seed: int = 0) -> dict:
    key_list = jax.random.split(jax.random.key(seed), 4)
    return {
        "base_flow": bell_draw(key_list[0], (3, NZ, NY, NX), 1.0, 6.0, ((1, 16),), jnp.float32),
        "tangents": bell_draw(key_list[1], (VECS, 3, NZ, NY, NX), 1.0, 6.0, ((0, 32), (2, 16)), jnp.float32),
        "shells": set_ends(jax.random.randint(key_list[2], (NFORCE,), 1, NZ // 4), jax.random.fold_in(key_list[2], 1), 1, (NZ // 4) - 1).astype(jnp.int32),
    }


time_step = 0.005
viscosity = 0.01
forcing_amplitude = 4.0
highest = lax.Precision.HIGHEST

def grid_spacing():
    return 2.0 * math.pi / NX

def central(field, axis):
    return (jnp.roll(field, -1, axis) - jnp.roll(field, 1, axis)) / (2.0 * grid_spacing())

def laplacian(field):
    spacing = grid_spacing()
    summed = -6.0 * field
    for axis in (-1, -2, -3):
        summed = summed + jnp.roll(field, -1, axis) + jnp.roll(field, 1, axis)
    return summed / (spacing * spacing)

def forcing_field(shells):
    positions = jnp.arange(NZ, dtype=jnp.int32)
    angles = 2.0 * math.pi / NZ * (shells[:, None] * positions[None, :] % NZ).astype(jnp.float32)
    profile = forcing_amplitude * jnp.sum(jnp.sin(angles), axis=0)
    first = jnp.broadcast_to(profile[:, None, None], (NZ, NY, NX))
    zeros = jnp.zeros((NZ, NY, NX), jnp.float32)
    return jnp.stack([first, zeros, zeros])

def wave_symbols():
    spacing = grid_spacing()
    wave_z = jnp.arange(NZ, dtype=jnp.int32)[:, None, None]
    wave_y = jnp.arange(NY, dtype=jnp.int32)[None, :, None]
    wave_x = jnp.arange(NX, dtype=jnp.int32)[None, None, :]

    def slope(wave, length):
        return jnp.sin(2.0 * math.pi / length * wave.astype(jnp.float32)) / spacing
    shape = (NZ, NY, NX)
    vectors = jnp.stack([jnp.broadcast_to(slope(wave_x, NX), shape), jnp.broadcast_to(slope(wave_y, NY), shape), jnp.broadcast_to(slope(wave_z, NZ), shape)])
    resting = (wave_x % (NX // 2) == 0) & (wave_y % (NY // 2) == 0) & (wave_z % (NZ // 2) == 0)
    squared = jnp.sum(vectors * vectors, axis=0)
    inverse = jnp.where(resting, 0.0, 1.0 / jnp.where(resting, 1.0, squared))
    return (vectors, inverse)

def project(rates):
    vectors, inverse = wave_symbols()
    spectrum = jnp.fft.fftn(rates, axes=(1, 2, 3))
    normal_part = jnp.sum(vectors * spectrum, axis=0, keepdims=True)
    return jnp.real(jnp.fft.ifftn(spectrum - vectors * normal_part * inverse, axes=(1, 2, 3))).astype(jnp.float32)

def base_rate(velocity, forcing):
    advect = velocity[0][None] * central(velocity, -1)
    advect = advect + velocity[1][None] * central(velocity, -2)
    advect = advect + velocity[2][None] * central(velocity, -3)
    return -advect + viscosity * laplacian(velocity) + forcing

def tangent_rate(tangent, velocity):
    advect = jnp.zeros_like(tangent)
    for direction in range(3):
        axis = -1 - direction
        advect = advect + velocity[direction][None] * central(tangent, axis)
        advect = advect + tangent[direction][None] * central(velocity, axis)
    return -advect + viscosity * laplacian(tangent)

def reference(base_flow, tangents, shells):
    forcing = forcing_field(shells)
    base_next = base_flow + time_step * project(base_rate(base_flow, forcing))

    def advance_one(tangent):
        return tangent + time_step * project(tangent_rate(tangent, base_flow))
    advanced = lax.map(advance_one, tangents)
    flattened = advanced.reshape(advanced.shape[0], -1)
    gram_matrix = jnp.dot(flattened, flattened.T, precision=highest) / flattened.shape[1]
    factor = jnp.linalg.cholesky(gram_matrix)
    ortho_rows = lax.linalg.triangular_solve(factor, flattened, left_side=True, lower=True)
    return (base_next, ortho_rows.reshape(tangents.shape), jnp.log(jnp.diagonal(factor)))
```

```python
import functools
import math

import jax
import jax.numpy as jnp
import numpy as np
from jax import lax
from jax.experimental import pallas as pl
from jax.experimental.pallas import tpu as pltpu
from jax.sharding import PartitionSpec as P

N = 128
GZ = 16
NV = 32
LZ = N // GZ
ROWS = 3 * LZ * N // NV
time_step = 0.005
viscosity = 0.01
forcing_amplitude = 4.0
spacing = 2.0 * math.pi / N
half_inv = 1.0 / (2.0 * spacing)
lap_scale = viscosity / (spacing * spacing)
f32, bf16 = jnp.float32, jnp.bfloat16
MESH = pl.DeviceIdType.MESH


def tables():
    k = np.arange(N)
    angle = 2.0 * np.pi / N * ((k[:, None] * k[None, :]) % N)
    c, s = np.cos(angle), np.sin(angle)
    a = np.block([[c, -s], [s, c]]).astype(np.float32)
    hi = a.astype(jnp.bfloat16)
    lo = (a - hi.astype(np.float32)).astype(jnp.bfloat16)
    sine = np.sin(2.0 * np.pi / N * k)
    sine[[0, 64]] = 0.0
    slope2 = ((sine / spacing) ** 2).astype(np.float32)
    return hi, lo, np.ascontiguousarray(hi.T), np.ascontiguousarray(lo.T), sine.astype(np.float32), slope2


def split(x):
    hi = x.astype(bf16)
    return hi, (x - hi.astype(f32)).astype(bf16)


def dot(a, b):
    return jnp.dot(a, b, preferred_element_type=f32)


def right(x, hi, lo):
    xh, xl = split(x)
    return dot(xh, hi) + (dot(xl, hi) + dot(xh, lo))


def left(hi, lo, x):
    xh, xl = split(x)
    return dot(hi, xh) + (dot(hi, xl) + dot(lo, xh))


def up(x, axis):
    return pltpu.roll(x, N - 1, axis)


def down(x, axis):
    return pltpu.roll(x, 1, axis)


def kernel(shells, sine, base, tang, ahi, alo, bhi, blo, s2row, s2col,
           base_out, ortho, growth,
           E, Rt, S, T, T2, S2, Pf, V, BN, R, X, O2, gbuf, gsend, grecv, vsend, vrecv,
           lsem, hs, hr, a1s, a1r, a2s, a2r, ps, pr, vs, vr, gs, gr, ws, wr, os_, or_):
    v = lax.axis_index("vec")
    g = lax.axis_index("gz")
    nxt = lax.rem(g + 1, GZ)
    prv = lax.rem(g + GZ - 1, GZ)

    def zpeer(i):
        return lax.rem(g + i, GZ)

    def vpeer(i):
        return lax.rem(v + i, NV)

    barrier = pltpu.get_barrier_semaphore()

    @pl.loop(1, GZ)
    def _(i):
        pl.semaphore_signal(barrier, inc=1, device_id=(v, zpeer(i)), device_id_type=MESH)

    @pl.loop(1, NV)
    def _(i):
        pl.semaphore_signal(barrier, inc=1, device_id=(vpeer(i), g), device_id_type=MESH)

    load0 = pltpu.make_async_copy(base, E.at[0:3, 2:10], lsem.at[0])
    load1 = pltpu.make_async_copy(tang, E.at[3:6, 2:10], lsem.at[1])
    load0.start()
    load1.start()
    pl.semaphore_wait(barrier, GZ + NV - 2)

    halos = []
    for f, src in ((0, base), (3, tang)):
        for who, a, b in ((nxt, (LZ - 1, LZ - 2), (1, 0)), (prv, (0, 0), (10, 10))):
            n = len(halos)
            halos.append(pltpu.make_async_remote_copy(
                src.at[0:2, a[0]:a[0] + 1], E.at[f:f + 2, b[0]:b[0] + 1],
                hs.at[n], hr.at[n], device_id=(v, who), device_id_type=MESH))
            n += 1
            halos.append(pltpu.make_async_remote_copy(
                src.at[2, a[1]:a[1] + 2], E.at[f + 2, b[1]:b[1] + 2],
                hs.at[n], hr.at[n], device_id=(v, who), device_id_type=MESH))
    for h in halos:
        h.start()
    load0.wait()
    load1.wait()

    def rates(e, comps):
        bx, by, bz = E[0, e], E[1, e], E[2, e]
        tx, ty, tz = E[3, e], E[4, e], E[5, e]
        for c in comps:
            f = E[c, e]
            xp, xm, yp, ym, zp, zm = up(f, 1), down(f, 1), up(f, 0), down(f, 0), E[c, e + 1], E[c, e - 1]
            dx, dy, dz = xp - xm, yp - ym, zp - zm
            if comps != (2,):
                pass
            lap = ((xp + xm) + (yp + ym)) + (zp + zm) - 6.0 * f
            brate = lap * lap_scale - (bx * dx + by * dy + bz * dz) * half_inv
            if c == 0:
                zz = g * LZ + (e - 2)
                prof = 0.0
                for j in range(4):
                    prof = prof + sine[lax.rem(shells[j] * zz, N)]
                brate = brate + prof * forcing_amplitude
            Rt[c, e - 1] = brate
            adv = tx * dx + ty * dy + tz * dz
            f = E[c + 3, e]
            xp, xm, yp, ym, zp, zm = up(f, 1), down(f, 1), up(f, 0), down(f, 0), E[c + 3, e + 1], E[c + 3, e - 1]
            lap = ((xp + xm) + (yp + ym)) + (zp + zm) - 6.0 * f
            adv = adv + (bx * (xp - xm) + by * (yp - ym) + bz * (zp - zm))
            Rt[c + 3, e - 1] = lap * lap_scale - adv * half_inv

    @pl.loop(3, 9)
    def _(e):
        rates(e, (0, 1, 2))

    for h in halos:
        h.wait()

    @pl.loop(0, 2)
    def _(i):
        rates(2 + 7 * i, (0, 1, 2))

    @pl.loop(0, 2)
    def _(i):
        rates(1 + 9 * i, (2,))

    @pl.loop(0, LZ // 2)
    def _(p):
        parts = []
        for q in range(2):
            r = 2 * p + q + 1
            div = []
            for f in (0, 3):
                rx, ry = Rt[f, r], Rt[f + 1, r]
                d = (up(rx, 1) - down(rx, 1)) + (up(ry, 0) - down(ry, 0)) + (Rt[f + 2, r + 1] - Rt[f + 2, r - 1])
                div.append(d * half_inv)
            parts.append(right(jnp.concatenate(div, axis=1), ahi[...], alo[...]))
        rhs = jnp.concatenate([
            jnp.concatenate([parts[0][:, :N], parts[1][:, :N]], axis=1),
            jnp.concatenate([parts[0][:, N:], parts[1][:, N:]], axis=1)], axis=0)
        y = left(bhi[...], blo[...], rhs)
        for q in range(2):
            z8 = pl.multiple_of((2 * p + q) * 8, 8)
            for r in range(2):
                S[:, r, pl.ds(z8, 8), :] = y[r * N:(r + 1) * N, q * N:(q + 1) * N].reshape(GZ, 8, N)

    def a2a1(i):
        p = zpeer(i)
        return pltpu.make_async_remote_copy(
            S.at[p], T.at[:, pl.ds(pl.multiple_of(g * 64, 64), 64), :],
            a1s.at[i], a1r.at[i], device_id=(v, p), device_id_type=MESH)

    @pl.loop(1, GZ)
    def _(i):
        a2a1(i).start()

    own = pltpu.make_async_copy(S.at[g], T.at[:, pl.ds(pl.multiple_of(g * 64, 64), 64), :], lsem.at[0])
    own.start()
    own.wait()

    @pl.loop(1, GZ)
    def _(i):
        a2a1(i).wait()

    @pl.loop(0, 4)
    def _(p):
        blocks = [[T[r, pl.ds(2 * p + q, N, stride=8), :] for q in range(2)] for r in range(2)]
        rhs = jnp.concatenate([jnp.concatenate(b, axis=1) for b in blocks], axis=0)
        y = left(bhi[...], blo[...], rhs)
        kz = lax.broadcasted_iota(jnp.int32, (N, N), 0)
        kx = lax.broadcasted_iota(jnp.int32, (N, N), 1)
        qs = []
        for q in range(2):
            ky = g * 8 + 2 * p + q
            rest = (lax.rem(kz, 64) == 0) & (lax.rem(kx, 64) == 0) & (lax.rem(ky, 64) == 0)
            sq = s2col[...] + (s2row[...] + s2col[pl.ds(ky, 1), :])
            qs.append(jnp.where(rest, 0.0, (-1.0 / (N * N * N)) / jnp.where(rest, 1.0, sq)))
        qq = jnp.concatenate(qs, axis=1)
        y = jnp.concatenate([y[:N] * qq, y[N:] * qq], axis=0)
        y = left(ahi[...], alo[...], y)
        for r in range(2):
            for q in range(2):
                T2[r, pl.ds(2 * p + q, N, stride=8), :] = y[r * N:(r + 1) * N, q * N:(q + 1) * N]

    def a2a2(i):
        p = zpeer(i)
        return pltpu.make_async_remote_copy(
            T2.at[:, pl.ds(pl.multiple_of(p * 64, 64), 64), :], S2.at[g],
            a2s.at[i], a2r.at[i], device_id=(v, p), device_id_type=MESH)

    @pl.loop(1, GZ)
    def _(i):
        a2a2(i).start()

    own = pltpu.make_async_copy(T2.at[:, pl.ds(pl.multiple_of(g * 64, 64), 64), :], S2.at[g], lsem.at[1])
    own.start()
    own.wait()

    @pl.loop(1, GZ)
    def _(i):
        a2a2(i).wait()

    @pl.loop(0, LZ // 2)
    def _(p):
        blocks = []
        for r in range(2):
            blocks.append(jnp.concatenate(
                [S2[:, r, pl.ds(pl.multiple_of((2 * p + q) * 8, 8), 8), :].reshape(N, N) for q in range(2)], axis=1))
        y = left(ahi[...], alo[...], jnp.concatenate(blocks, axis=0))
        for q in range(2):
            c = jnp.concatenate([y[:N, q * N:(q + 1) * N], y[N:, q * N:(q + 1) * N]], axis=1)
            phi = right(c, bhi[...], blo[...])
            Pf[0, 2 * p + q + 1] = phi[:, :N]
            Pf[1, 2 * p + q + 1] = phi[:, N:]

    edge0 = pltpu.make_async_remote_copy(
        Pf.at[:, LZ:LZ + 1], Pf.at[:, 0:1], ps.at[0], pr.at[0], device_id=(v, nxt), device_id_type=MESH)
    edge1 = pltpu.make_async_remote_copy(
        Pf.at[:, 1:2], Pf.at[:, LZ + 1:LZ + 2], ps.at[1], pr.at[1], device_id=(v, prv), device_id_type=MESH)
    edge0.start()
    edge1.start()

    def correct(z):
        for s in range(2):
            phi = Pf[s, z + 1]
            grads = (up(phi, 1) - down(phi, 1), up(phi, 0) - down(phi, 0), Pf[s, z + 2] - Pf[s, z])
            for c in range(3):
                out = E[3 * s + c, z + 2] + time_step * (Rt[3 * s + c, z + 1] - grads[c] * half_inv)
                if s == 0:
                    BN[c, z] = out
                else:
                    V[pl.ds(pl.multiple_of((c * LZ + z) * N, N), N), :] = out

    @pl.loop(1, LZ - 1)
    def _(z):
        correct(z)

    edge0.wait()
    edge1.wait()

    @pl.loop(0, 2)
    def _(i):
        correct((LZ - 1) * i)

    def a2a3(i):
        p = vpeer(i)
        return pltpu.make_async_remote_copy(
            V.at[pl.ds(pl.multiple_of(p * ROWS, 8), ROWS)], R.at[pl.ds(pl.multiple_of(v * ROWS, 8), ROWS)],
            vs.at[i], vr.at[i], device_id=(p, g), device_id_type=MESH)

    @pl.loop(1, NV)
    def _(i):
        a2a3(i).start()

    mine = pl.multiple_of(v * ROWS, 8)
    own = pltpu.make_async_copy(V.at[pl.ds(mine, ROWS)], R.at[pl.ds(mine, ROWS)], lsem.at[0])
    own.start()

    y8 = pl.multiple_of((v // 2) * 8, 8)
    odd = lax.rem(v, 2) == 1

    @pl.loop(0, LZ)
    def _(z):
        for c in range(3):
            blk = BN[c, z, pl.ds(y8, 8), :]
            base_out[c, z] = jnp.where(odd, blk[4:8], blk[0:4])

    own.wait()

    @pl.loop(1, NV)
    def _(i):
        a2a3(i).wait()

    def gram_step(k, acc):
        cols = [R[pl.ds(8 * k + j, NV, stride=ROWS), :] for j in range(8)]
        x = jnp.concatenate(cols, axis=1)
        X[k] = x
        return acc + lax.dot_general(x, x, (((1,), (1,)), ((), ())), precision=lax.Precision.HIGHEST,
                                     preferred_element_type=f32)

    gram = lax.fori_loop(0, ROWS // 8, gram_step, jnp.zeros((NV, NV), f32))
    gbuf[...] = jnp.zeros((NV, N), f32)
    gbuf[:, 0:NV] = gram
    full = gbuf[...]
    packed = full[0:8]
    for b in range(1, 4):
        packed = packed + pltpu.roll(full[8 * b:8 * b + 8], 32 * b, 1)

    gsend[...] = packed
    grecv[g] = packed

    def ex1(i):
        return pltpu.make_async_remote_copy(
            gsend, grecv.at[g], gs.at[i], gr.at[i], device_id=(v, zpeer(i)), device_id_type=MESH)

    @pl.loop(1, GZ)
    def _(i):
        ex1(i).start()

    @pl.loop(1, GZ)
    def _(i):
        ex1(i).wait()

    total = grecv[0]
    for i in range(1, GZ):
        total = total + grecv[i]
    vsend[...] = total
    vrecv[v] = total

    def ex2(i):
        return pltpu.make_async_remote_copy(
            vsend, vrecv.at[v], ws.at[i], wr.at[i], device_id=(vpeer(i), g), device_id_type=MESH)

    @pl.loop(1, NV)
    def _(i):
        ex2(i).start()

    @pl.loop(1, NV)
    def _(i):
        ex2(i).wait()

    total = vrecv[0]
    for i in range(1, NV):
        total = total + vrecv[i]
    total = total / (3.0 * N * N * N)
    lane = lax.broadcasted_iota(jnp.int32, (NV, N), 1)
    row = lax.broadcasted_iota(jnp.int32, (NV, N), 0)
    m = jnp.concatenate([total] + [pltpu.roll(total, N - 32 * b, 1) for b in range(1, 4)], axis=0)
    m = jnp.where(lane < NV, m, jnp.where(lane == row + NV, 1.0, 0.0))
    for k in range(NV - 1):
        col = jnp.broadcast_to(m[:, k:k + 1], (NV, N))
        prow = m[k:k + 1, :]
        piv = col[k:k + 1, :]
        fac = jnp.where(row > k, col * (1.0 / piv), 0.0)
        m = m - fac * prow
    diag = jnp.where(lane == row, m, 0.0)
    dcol = jnp.sum(diag, axis=1, keepdims=True)
    drow = jnp.sum(diag, axis=0, keepdims=True)
    growth[...] = 0.5 * jnp.log(drow[:, 0:NV])
    inv = pltpu.roll(m, N - NV, 1) * (1.0 / jnp.sqrt(dcol))
    inv = inv[:, 0:NV]

    @pl.loop(0, ROWS // 8)
    def _(k):
        o = lax.dot_general(inv, X[k], (((1,), (0,)), ((), ())), precision=lax.Precision.HIGHEST,
                            preferred_element_type=f32)
        for j in range(8):
            O2[pl.ds(8 * k + j, NV, stride=ROWS), :] = o[:, j * N:(j + 1) * N]

    def a2a4(i):
        p = vpeer(i)
        return pltpu.make_async_remote_copy(
            O2.at[pl.ds(pl.multiple_of(p * ROWS, 8), ROWS)], ortho.at[pl.ds(pl.multiple_of(v * ROWS, 8), ROWS)],
            os_.at[i], or_.at[i], device_id=(p, g), device_id_type=MESH)

    @pl.loop(1, NV)
    def _(i):
        a2a4(i).start()

    own = pltpu.make_async_copy(O2.at[pl.ds(mine, ROWS)], ortho.at[pl.ds(mine, ROWS)], lsem.at[1])
    own.start()
    own.wait()

    @pl.loop(1, NV)
    def _(i):
        a2a4(i).wait()


def per_device(base_flow, tangents, shells):
    ahi, alo, bhi, blo, sine, slope2 = tables()
    vm = pl.BlockSpec(memory_space=pltpu.VMEM)
    sm = pl.BlockSpec(memory_space=pltpu.SMEM)
    anyspace = pl.BlockSpec(memory_space=pl.ANY)
    dma = pltpu.SemaphoreType.DMA
    plane = (N, N)
    base_rows, ortho, growth = pl.pallas_call(
        kernel,
        out_shape=(
            jax.ShapeDtypeStruct((3, LZ, N // NV, N), f32),
            jax.ShapeDtypeStruct((3 * LZ * N, N), f32),
            jax.ShapeDtypeStruct((1, NV), f32),
        ),
        in_specs=[sm, sm, anyspace, anyspace, vm, vm, vm, vm, vm, vm],
        out_specs=(vm, anyspace, vm),
        scratch_shapes=[
            pltpu.VMEM((6, 12) + plane, f32),
            pltpu.VMEM((6, 10) + plane, f32),
            pltpu.VMEM((GZ, 2, 64, N), f32),
            pltpu.VMEM((2, 1024, N), f32),
            pltpu.VMEM((2, 1024, N), f32),
            pltpu.VMEM((GZ, 2, 64, N), f32),
            pltpu.VMEM((2, LZ + 2) + plane, f32),
            pltpu.VMEM((3 * LZ * N, N), f32),
            pltpu.VMEM((3, LZ) + plane, f32),
            pltpu.VMEM((3 * LZ * N, N), f32),
            pltpu.VMEM((ROWS // 8, NV, 8 * N), f32),
            pltpu.VMEM((3 * LZ * N, N), f32),
            pltpu.VMEM((NV, N), f32),
            pltpu.VMEM((8, N), f32),
            pltpu.VMEM((GZ, 8, N), f32),
            pltpu.VMEM((8, N), f32),
            pltpu.VMEM((NV, 8, N), f32),
            dma((2,)),
            dma((8,)), dma((8,)),
            dma((GZ,)), dma((GZ,)),
            dma((GZ,)), dma((GZ,)),
            dma((2,)), dma((2,)),
            dma((NV,)), dma((NV,)),
            dma((GZ,)), dma((GZ,)),
            dma((NV,)), dma((NV,)),
            dma((NV,)), dma((NV,)),
        ],
        compiler_params=pltpu.CompilerParams(
            collective_id=0, has_side_effects=True, vmem_limit_bytes=58 * 1024 * 1024
        ),
    )(
        shells, jnp.asarray(sine), base_flow, tangents[0],
        jnp.asarray(ahi), jnp.asarray(alo), jnp.asarray(bhi), jnp.asarray(blo),
        jnp.broadcast_to(jnp.asarray(slope2)[None, :], (1, N)),
        jnp.broadcast_to(jnp.asarray(slope2)[:, None], (N, N)),
    )
    return base_rows, ortho.reshape(tangents.shape), growth[0]


def solution(mesh):
    in_specs = (P(None, "gz", None, None), P("vec", None, "gz", None, None), P())
    out_specs = (P(None, "gz", "vec", None), P("vec", None, "gz", None, None), P())
    return jax.shard_map(
        per_device, mesh=mesh, in_specs=in_specs, out_specs=out_specs, check_vma=False
    )
```

```python
import functools
import math

import jax
import jax.numpy as jnp
import numpy as np
from jax import lax
from jax.experimental import pallas as pl
from jax.experimental.pallas import tpu as pltpu
from jax.sharding import PartitionSpec as P

N = 128
GZ = 16
NV = 32
LZ = N // GZ
ROWS = 3 * LZ * N // NV
time_step = 0.005
viscosity = 0.01
forcing_amplitude = 4.0
spacing = 2.0 * math.pi / N
half_inv = 1.0 / (2.0 * spacing)
lap_scale = viscosity / (spacing * spacing)
f32, bf16 = jnp.float32, jnp.bfloat16
MESH = pl.DeviceIdType.MESH


def tables():
    k = np.arange(N)
    angle = 2.0 * np.pi / N * ((k[:, None] * k[None, :]) % N)
    c, s = np.cos(angle), np.sin(angle)
    a = np.block([[c, -s], [s, c]]).astype(np.float32)
    hi = a.astype(jnp.bfloat16)
    lo = (a - hi.astype(np.float32)).astype(jnp.bfloat16)
    sine = np.sin(2.0 * np.pi / N * k)
    sine[[0, 64]] = 0.0
    slope2 = ((sine / spacing) ** 2).astype(np.float32)
    return hi, lo, np.ascontiguousarray(hi.T), np.ascontiguousarray(lo.T), sine.astype(np.float32), slope2


def split(x):
    hi = x.astype(bf16)
    return hi, (x - hi.astype(f32)).astype(bf16)


def dot(a, b):
    return jnp.dot(a, b, preferred_element_type=f32)


def right(x, hi, lo):
    xh, xl = split(x)
    return dot(xh, hi) + (dot(xl, hi) + dot(xh, lo))


def left(hi, lo, x):
    xh, xl = split(x)
    return dot(hi, xh) + (dot(hi, xl) + dot(lo, xh))


def up(x, axis):
    return pltpu.roll(x, N - 1, axis)


def down(x, axis):
    return pltpu.roll(x, 1, axis)


def kernel(shells, sine, base, tang, ahi, alo, bhi, blo, s2row, s2col,
           base_out, ortho, growth,
           E, Rt, S, T, T2, S2, Pf, YS, BN, R, PS, RE, hsend, hrecv, HB, V2, X, O2, O5, gbuf, gsend, grecv, vsend, vrecv,
           lsem, hs, hr, a1s, a1r, a2s, a2r, ps, pr, ys, yr, es, er, fs, fr, ns, nr, gs, gr, ws, wr, os_, or_):
    v = lax.axis_index("vec")
    g = lax.axis_index("gz")
    nxt = lax.rem(g + 1, GZ)
    prv = lax.rem(g + GZ - 1, GZ)
    half = v // 16
    ring = lax.rem(v, 16)
    other = (1 - half) * 16 + ring

    def zpeer(i):
        return lax.rem(g + i, GZ)

    def vpeer(i):
        return lax.rem(half + i // 16, 2) * 16 + lax.rem(ring + i, 16)

    barrier = pltpu.get_barrier_semaphore()

    @pl.loop(1, GZ)
    def _(i):
        pl.semaphore_signal(barrier, inc=1, device_id=(v, zpeer(i)), device_id_type=MESH)

    @pl.loop(1, NV)
    def _(i):
        pl.semaphore_signal(barrier, inc=1, device_id=(vpeer(i), g), device_id_type=MESH)

    above = (other, lax.rem(g + half, GZ))
    below = (other, lax.rem(g + GZ - 1 + half, GZ))
    diagonal = (other, lax.rem(g + GZ - 1 + 2 * half, GZ))
    pl.semaphore_signal(barrier, inc=1, device_id=diagonal, device_id_type=MESH)

    load0 = pltpu.make_async_copy(base, E.at[0:3, 2:10], lsem.at[0])
    load1 = pltpu.make_async_copy(tang, E.at[3:6, 2:10], lsem.at[1])
    load0.start()
    load1.start()
    load0.wait()
    load1.wait()

    def rates(e, comps):
        bx, by, bz = E[0, e], E[1, e], E[2, e]
        tx, ty, tz = E[3, e], E[4, e], E[5, e]
        for c in comps:
            f = E[c, e]
            xp, xm, yp, ym, zp, zm = up(f, 1), down(f, 1), up(f, 0), down(f, 0), E[c, e + 1], E[c, e - 1]
            dx, dy, dz = xp - xm, yp - ym, zp - zm
            lap = ((xp + xm) + (yp + ym)) + (zp + zm) - 6.0 * f
            brate = lap * lap_scale - (bx * dx + by * dy + bz * dz) * half_inv
            if c == 0:
                zz = g * LZ + (e - 2)
                prof = 0.0
                for j in range(4):
                    prof = prof + sine[lax.rem(shells[j] * zz, N)]
                brate = brate + prof * forcing_amplitude
            Rt[c, e - 1] = brate
            adv = tx * dx + ty * dy + tz * dz
            f = E[c + 3, e]
            xp, xm, yp, ym, zp, zm = up(f, 1), down(f, 1), up(f, 0), down(f, 0), E[c + 3, e + 1], E[c + 3, e - 1]
            lap = ((xp + xm) + (yp + ym)) + (zp + zm) - 6.0 * f
            adv = adv + (bx * (xp - xm) + by * (yp - ym) + bz * (zp - zm))
            trate = lap * lap_scale - adv * half_inv
            Rt[c + 3, e - 1] = trate
            if len(comps) == 3:
                z = e - 2
                YS[pl.ds((z // 4) * 16, 16), c, lax.rem(z, 4)] = (f + time_step * trate).reshape(16, 8, N)

    @pl.loop(3, 9)
    def _(e):
        rates(e, (0, 1, 2))

    pl.semaphore_wait(barrier, GZ + NV - 1)

    halos = []
    for f, src in ((3, tang), (0, base)):
        for who, a, b in ((nxt, (LZ - 1, LZ - 2), (1, 0)), (prv, (0, 0), (10, 10))):
            n = len(halos)
            halos.append(pltpu.make_async_remote_copy(
                src.at[0:2, a[0]:a[0] + 1], E.at[f:f + 2, b[0]:b[0] + 1],
                hs.at[n], hr.at[n], device_id=(v, who), device_id_type=MESH))
            n += 1
            halos.append(pltpu.make_async_remote_copy(
                src.at[2, a[1]:a[1] + 2], E.at[f + 2, b[1]:b[1] + 2],
                hs.at[n], hr.at[n], device_id=(v, who), device_id_type=MESH))
    for h in halos:
        h.start()

    def inner(i):
        p = vpeer(i)
        z = 1 - p // 16
        return pltpu.make_async_remote_copy(
            YS.at[p, :, pl.ds(z, 3)], R.at[v, :, pl.ds(z, 3)],
            ys.at[i], yr.at[i], device_id=(p, g), device_id_type=MESH)

    def outer(i):
        p = vpeer(i)
        z = 3 * (p // 16)
        return pltpu.make_async_remote_copy(
            YS.at[p, :, z], R.at[v, :, z],
            es.at[i], er.at[i], device_id=(p, g), device_id_type=MESH)

    @pl.loop(1, NV)
    def _(i):
        inner(i).start()

    for h in halos:
        h.wait()

    @pl.loop(0, 2)
    def _(i):
        rates(2 + 7 * i, (0, 1, 2))

    @pl.loop(0, 2)
    def _(i):
        rates(1 + 9 * i, (2,))

    @pl.loop(0, LZ // 2)
    def _(p):
        parts = []
        for q in range(2):
            r = 2 * p + q + 1
            div = []
            for f in (0, 3):
                rx, ry = Rt[f, r], Rt[f + 1, r]
                d = (up(rx, 1) - down(rx, 1)) + (up(ry, 0) - down(ry, 0)) + (Rt[f + 2, r + 1] - Rt[f + 2, r - 1])
                div.append(d * half_inv)
            parts.append(right(jnp.concatenate(div, axis=1), ahi[...], alo[...]))
        rhs = jnp.concatenate([
            jnp.concatenate([parts[0][:, :N], parts[1][:, :N]], axis=1),
            jnp.concatenate([parts[0][:, N:], parts[1][:, N:]], axis=1)], axis=0)
        y = left(bhi[...], blo[...], rhs)
        for q in range(2):
            z8 = pl.multiple_of((2 * p + q) * 8, 8)
            for r in range(2):
                S[:, r, pl.ds(z8, 8), :] = y[r * N:(r + 1) * N, q * N:(q + 1) * N].reshape(GZ, 8, N)

    def a2a1(i):
        p = zpeer(i)
        return pltpu.make_async_remote_copy(
            S.at[p], T.at[:, pl.ds(pl.multiple_of(g * 64, 64), 64), :],
            a1s.at[i], a1r.at[i], device_id=(v, p), device_id_type=MESH)

    @pl.loop(1, GZ)
    def _(i):
        a2a1(i).start()

    @pl.loop(1, NV)
    def _(i):
        outer(i).start()

    keep = pltpu.make_async_copy(YS.at[v], R.at[v], lsem.at[2])
    keep.start()
    own = pltpu.make_async_copy(S.at[g], T.at[:, pl.ds(pl.multiple_of(g * 64, 64), 64), :], lsem.at[0])
    own.start()
    own.wait()

    @pl.loop(1, GZ)
    def _(i):
        a2a1(i).wait()

    @pl.loop(0, 4)
    def _(p):
        blocks = [[T[r, pl.ds(2 * p + q, N, stride=8), :] for q in range(2)] for r in range(2)]
        rhs = jnp.concatenate([jnp.concatenate(b, axis=1) for b in blocks], axis=0)
        y = left(bhi[...], blo[...], rhs)
        kz = lax.broadcasted_iota(jnp.int32, (N, N), 0)
        kx = lax.broadcasted_iota(jnp.int32, (N, N), 1)
        qs = []
        for q in range(2):
            ky = g * 8 + 2 * p + q
            rest = (lax.rem(kz, 64) == 0) & (lax.rem(kx, 64) == 0) & (lax.rem(ky, 64) == 0)
            sq = s2col[...] + (s2row[...] + s2col[pl.ds(ky, 1), :])
            qs.append(jnp.where(rest, 0.0, (-1.0 / (N * N * N)) / jnp.where(rest, 1.0, sq)))
        qq = jnp.concatenate(qs, axis=1)
        y = jnp.concatenate([y[:N] * qq, y[N:] * qq], axis=0)
        y = left(ahi[...], alo[...], y)
        for r in range(2):
            for q in range(2):
                T2[r, pl.ds(2 * p + q, N, stride=8), :] = y[r * N:(r + 1) * N, q * N:(q + 1) * N]

    def a2a2(i):
        p = zpeer(i)
        return pltpu.make_async_remote_copy(
            T2.at[:, pl.ds(pl.multiple_of(p * 64, 64), 64), :], S2.at[g],
            a2s.at[i], a2r.at[i], device_id=(v, p), device_id_type=MESH)

    @pl.loop(1, GZ)
    def _(i):
        a2a2(i).start()

    own = pltpu.make_async_copy(T2.at[:, pl.ds(pl.multiple_of(g * 64, 64), 64), :], S2.at[g], lsem.at[1])
    own.start()
    own.wait()

    @pl.loop(1, GZ)
    def _(i):
        a2a2(i).wait()

    @pl.loop(0, LZ // 2)
    def _(p):
        blocks = []
        for r in range(2):
            blocks.append(jnp.concatenate(
                [S2[:, r, pl.ds(pl.multiple_of((2 * p + q) * 8, 8), 8), :].reshape(N, N) for q in range(2)], axis=1))
        y = left(ahi[...], alo[...], jnp.concatenate(blocks, axis=0))
        for q in range(2):
            c = jnp.concatenate([y[:N, q * N:(q + 1) * N], y[N:, q * N:(q + 1) * N]], axis=1)
            phi = right(c, bhi[...], blo[...])
            z = 2 * p + q
            Pf[z + 1] = phi[:, :N]
            PS[pl.ds((z // 4) * 16, 16), lax.rem(z, 4)] = phi[:, N:].reshape(16, 8, N)

    def phis(i):
        p = vpeer(i)
        return pltpu.make_async_remote_copy(
            PS.at[p], RE.at[v, 1:5], fs.at[i], fr.at[i], device_id=(p, g), device_id_type=MESH)

    @pl.loop(1, NV)
    def _(i):
        phis(i).start()

    mine = pltpu.make_async_copy(PS.at[v], RE.at[v, 1:5], lsem.at[0])
    mine.start()

    y8 = pl.multiple_of((v // 2) * 8, 8)
    odd = lax.rem(v, 2) == 1
    edge0 = pltpu.make_async_remote_copy(
        Pf.at[LZ, pl.ds(y8, 8)], Pf.at[0, pl.ds(y8, 8)], ps.at[0], pr.at[0], device_id=(v, nxt), device_id_type=MESH)
    edge1 = pltpu.make_async_remote_copy(
        Pf.at[1, pl.ds(y8, 8)], Pf.at[LZ + 1, pl.ds(y8, 8)], ps.at[1], pr.at[1], device_id=(v, prv), device_id_type=MESH)
    edge0.start()
    edge1.start()

    @pl.loop(0, LZ)
    def _(z):
        phi = Pf[z + 1]
        BN[0, z] = up(phi, 1) - down(phi, 1)
        BN[1, z] = up(phi, 0) - down(phi, 0)

    edge0.wait()
    edge1.wait()

    @pl.loop(0, LZ)
    def _(z):
        rows = pl.ds(y8, 8)
        grads = (BN[0, z, rows], BN[1, z, rows], Pf[z + 2, rows] - Pf[z, rows])
        for c in range(3):
            blk = E[c, z + 2, rows] + time_step * (Rt[c, z + 1, rows] - grads[c] * half_inv)
            base_out[c, z] = jnp.where(odd, blk[4:8], blk[0:4])

    mine.wait()

    @pl.loop(1, NV)
    def _(i):
        phis(i).wait()

    for z in range(4):
        hsend[0, z * NV:(z + 1) * NV] = RE[:, z + 1, 7, :]
        hsend[1, z * NV:(z + 1) * NV] = RE[:, z + 1, 0, :]
    rimhi = half * 16 + lax.rem(ring + 1, 16)
    rimlo = half * 16 + lax.rem(ring + 15, 16)
    rims = [
        pltpu.make_async_remote_copy(hsend.at[0], hrecv.at[0], ns.at[0], nr.at[0], device_id=(rimhi, g), device_id_type=MESH),
        pltpu.make_async_remote_copy(hsend.at[1], hrecv.at[1], ns.at[1], nr.at[1], device_id=(rimlo, g), device_id_type=MESH),
        pltpu.make_async_remote_copy(RE.at[:, 4], RE.at[:, 0], ns.at[2], nr.at[2], device_id=above, device_id_type=MESH),
        pltpu.make_async_remote_copy(RE.at[:, 1], RE.at[:, 5], ns.at[3], nr.at[3], device_id=below, device_id_type=MESH),
    ]
    for c in rims:
        c.start()
    keep.wait()

    @pl.loop(1, NV)
    def _(i):
        inner(i).wait()

    @pl.loop(1, NV)
    def _(i):
        outer(i).wait()

    for c in rims:
        c.wait()
    HB[pl.ds(0, N, stride=8), :] = hrecv[0]
    HB[pl.ds(7, N, stride=8), :] = hrecv[1]
    sub = lax.broadcasted_iota(jnp.int32, (8, N), 0)

    @pl.loop(0, NV)
    def _(j):
        for z in range(4):
            phi = RE[j, z + 1]
            rim = HB[pl.ds(pl.multiple_of((z * NV + j) * 8, 8), 8), :]
            yp = jnp.where(sub == 7, rim, pltpu.roll(phi, 7, 0))
            ym = jnp.where(sub == 0, rim, pltpu.roll(phi, 1, 0))
            grads = (up(phi, 1) - down(phi, 1), yp - ym, RE[j, z + 2] - RE[j, z])
            for c in range(3):
                V2[pl.ds(pl.multiple_of(j * ROWS + c * 32 + z * 8, 8), 8), :] = (
                    R[j, c, z] - (time_step * half_inv) * grads[c])

    def gram_step(k, acc):
        cols = [V2[pl.ds(8 * k + j, NV, stride=ROWS), :] for j in range(8)]
        x = jnp.concatenate(cols, axis=1)
        X[k] = x
        return acc + lax.dot_general(x, x, (((1,), (1,)), ((), ())), precision=lax.Precision.HIGHEST,
                                     preferred_element_type=f32)

    gram = lax.fori_loop(0, ROWS // 8, gram_step, jnp.zeros((NV, NV), f32))
    gbuf[...] = jnp.zeros((NV, N), f32)
    gbuf[:, 0:NV] = gram
    full = gbuf[...]
    packed = full[0:8]
    for b in range(1, 4):
        packed = packed + pltpu.roll(full[8 * b:8 * b + 8], 32 * b, 1)

    gsend[...] = packed
    grecv[g] = packed

    def ex1(i):
        return pltpu.make_async_remote_copy(
            gsend, grecv.at[g], gs.at[i], gr.at[i], device_id=(v, zpeer(i)), device_id_type=MESH)

    @pl.loop(1, GZ)
    def _(i):
        ex1(i).start()

    @pl.loop(1, GZ)
    def _(i):
        ex1(i).wait()

    total = grecv[0]
    for i in range(1, GZ):
        total = total + grecv[i]
    vsend[...] = total
    vrecv[v] = total

    def ex2(i):
        return pltpu.make_async_remote_copy(
            vsend, vrecv.at[v], ws.at[i], wr.at[i], device_id=(vpeer(i), g), device_id_type=MESH)

    @pl.loop(1, NV)
    def _(i):
        ex2(i).start()

    @pl.loop(1, NV)
    def _(i):
        ex2(i).wait()

    total = vrecv[0]
    for i in range(1, NV):
        total = total + vrecv[i]
    total = total / (3.0 * N * N * N)
    lane = lax.broadcasted_iota(jnp.int32, (NV, N), 1)
    row = lax.broadcasted_iota(jnp.int32, (NV, N), 0)
    m = jnp.concatenate([total] + [pltpu.roll(total, N - 32 * b, 1) for b in range(1, 4)], axis=0)
    m = jnp.where(lane < NV, m, jnp.where(lane == row + NV, 1.0, 0.0))
    for k in range(NV - 1):
        col = jnp.broadcast_to(m[:, k:k + 1], (NV, N))
        prow = m[k:k + 1, :]
        piv = col[k:k + 1, :]
        fac = jnp.where(row > k, col * (1.0 / piv), 0.0)
        m = m - fac * prow
    diag = jnp.where(lane == row, m, 0.0)
    dcol = jnp.sum(diag, axis=1, keepdims=True)
    drow = jnp.sum(diag, axis=0, keepdims=True)
    growth[...] = 0.5 * jnp.log(drow[:, 0:NV])
    inv = pltpu.roll(m, N - NV, 1) * (1.0 / jnp.sqrt(dcol))
    inv = inv[:, 0:NV]

    @pl.loop(0, ROWS // 8)
    def _(k):
        o = lax.dot_general(inv, X[k], (((1,), (0,)), ((), ())), precision=lax.Precision.HIGHEST,
                            preferred_element_type=f32)
        for j in range(8):
            O2[pl.ds(8 * k + j, NV, stride=ROWS), :] = o[:, j * N:(j + 1) * N]

    @pl.loop(0, NV)
    def _(i):
        for c in range(3):
            for z in range(4):
                O5[i, c, z] = O2[pl.ds(pl.multiple_of(i * ROWS + c * 32 + z * 8, 8), 8), :]

    def a2a4(i):
        p = vpeer(i)
        return pltpu.make_async_remote_copy(
            O5.at[p], ortho.at[:, pl.ds(half * 4, 4), ring],
            os_.at[i], or_.at[i], device_id=(p, g), device_id_type=MESH)

    @pl.loop(1, NV)
    def _(i):
        a2a4(i).start()

    own = pltpu.make_async_copy(O5.at[v], ortho.at[:, pl.ds(half * 4, 4), ring], lsem.at[1])
    own.start()
    own.wait()

    @pl.loop(1, NV)
    def _(i):
        a2a4(i).wait()


def per_device(base_flow, tangents, shells):
    ahi, alo, bhi, blo, sine, slope2 = tables()
    vm = pl.BlockSpec(memory_space=pltpu.VMEM)
    sm = pl.BlockSpec(memory_space=pltpu.SMEM)
    anyspace = pl.BlockSpec(memory_space=pl.ANY)
    dma = pltpu.SemaphoreType.DMA
    plane = (N, N)
    base_rows, ortho, growth = pl.pallas_call(
        kernel,
        out_shape=(
            jax.ShapeDtypeStruct((3, LZ, N // NV, N), f32),
            jax.ShapeDtypeStruct((3, LZ, 16, 8, N), f32),
            jax.ShapeDtypeStruct((1, NV), f32),
        ),
        in_specs=[sm, sm, anyspace, anyspace, vm, vm, vm, vm, vm, vm],
        out_specs=(vm, anyspace, vm),
        scratch_shapes=[
            pltpu.VMEM((6, 12) + plane, f32),
            pltpu.VMEM((6, 10) + plane, f32),
            pltpu.VMEM((GZ, 2, 64, N), f32),
            pltpu.VMEM((2, 1024, N), f32),
            pltpu.VMEM((2, 1024, N), f32),
            pltpu.VMEM((GZ, 2, 64, N), f32),
            pltpu.VMEM((LZ + 2,) + plane, f32),
            pltpu.VMEM((NV, 3, 4, 8, N), f32),
            pltpu.VMEM((2, LZ) + plane, f32),
            pltpu.VMEM((NV, 3, 4, 8, N), f32),
            pltpu.VMEM((NV, 4, 8, N), f32),
            pltpu.VMEM((NV, 6, 8, N), f32),
            pltpu.VMEM((2,) + plane, f32),
            pltpu.VMEM((2,) + plane, f32),
            pltpu.VMEM((8 * N, N), f32),
            pltpu.VMEM((3 * LZ * N, N), f32),
            pltpu.VMEM((ROWS // 8, NV, 8 * N), f32),
            pltpu.VMEM((3 * LZ * N, N), f32),
            pltpu.VMEM((NV, 3, 4, 8, N), f32),
            pltpu.VMEM((NV, N), f32),
            pltpu.VMEM((8, N), f32),
            pltpu.VMEM((GZ, 8, N), f32),
            pltpu.VMEM((8, N), f32),
            pltpu.VMEM((NV, 8, N), f32),
            dma((3,)),
            dma((8,)), dma((8,)),
            dma((GZ,)), dma((GZ,)),
            dma((GZ,)), dma((GZ,)),
            dma((2,)), dma((2,)),
            dma((NV,)), dma((NV,)),
            dma((NV,)), dma((NV,)),
            dma((NV,)), dma((NV,)),
            dma((4,)), dma((4,)),
            dma((GZ,)), dma((GZ,)),
            dma((NV,)), dma((NV,)),
            dma((NV,)), dma((NV,)),
        ],
        compiler_params=pltpu.CompilerParams(
            collective_id=0, has_side_effects=True, vmem_limit_bytes=58 * 1024 * 1024
        ),
    )(
        shells, jnp.asarray(sine), base_flow, tangents[0],
        jnp.asarray(ahi), jnp.asarray(alo), jnp.asarray(bhi), jnp.asarray(blo),
        jnp.asarray(slope2[None, :]),
        jnp.asarray(np.repeat(slope2[:, None], N, axis=1)),
    )
    return base_rows, ortho.reshape(tangents.shape), growth[0]


def solution(mesh):
    in_specs = (P(None, "gz", None, None), P("vec", None, "gz", None, None), P())
    out_specs = (P(None, "gz", "vec", None), P("vec", None, "gz", None, None), P())
    return jax.shard_map(
        per_device, mesh=mesh, in_specs=in_specs, out_specs=out_specs, check_vma=False
    )
```

```python
import functools
import math

import jax
import jax.numpy as jnp
import numpy as np
from jax import lax
from jax.experimental import pallas as pl
from jax.experimental.pallas import tpu as pltpu
from jax.sharding import PartitionSpec as P

N = 128
GZ = 16
NV = 32
LZ = N // GZ
ROWS = 3 * LZ * N // NV
time_step = 0.005
viscosity = 0.01
forcing_amplitude = 4.0
spacing = 2.0 * math.pi / N
half_inv = 1.0 / (2.0 * spacing)
lap_scale = viscosity / (spacing * spacing)
f32, bf16 = jnp.float32, jnp.bfloat16
MESH = pl.DeviceIdType.MESH


def tables():
    k = np.arange(N)
    angle = 2.0 * np.pi / N * ((k[:, None] * k[None, :]) % N)
    c, s = np.cos(angle), np.sin(angle)
    a = np.block([[c, -s], [s, c]]).astype(np.float32)
    hi = a.astype(jnp.bfloat16)
    lo = (a - hi.astype(np.float32)).astype(jnp.bfloat16)
    sine = np.sin(2.0 * np.pi / N * k)
    sine[[0, 64]] = 0.0
    slope2 = ((sine / spacing) ** 2).astype(np.float32)
    lines = np.zeros((N + 16, N), np.float32)
    lines[:N] = slope2[:, None]
    lines[N] = slope2
    lines[N + 8] = sine
    return np.stack([hi, lo, hi.T, lo.T]), lines


def split(x):
    hi = x.astype(bf16)
    return hi, (x - hi.astype(f32)).astype(bf16)


def dot(a, b):
    return jnp.dot(a, b, preferred_element_type=f32)


def right(x, hi, lo):
    xh, xl = split(x)
    return dot(xh, hi) + (dot(xl, hi) + dot(xh, lo))


def left(hi, lo, x):
    xh, xl = split(x)
    return dot(hi, xh) + (dot(hi, xl) + dot(lo, xh))


def up(x, axis):
    return pltpu.roll(x, N - 1, axis)


def down(x, axis):
    return pltpu.roll(x, 1, axis)


def kernel(shells_in, base, tang, dft_in, lines_in,
           base_out, ortho, growth,
           shells, dft, lines, E, Rt, S, T, T2, S2, Pf, YS, BN, R, PS, RE, hsend, hrecv, HB, V2, X, O5, gbuf, gsend, grecv, vsend, vrecv,
           lsem, hs, hr, a1s, a1r, a2s, a2r, ps, pr, xs, xr, ys, yr, es, er, fs, fr, f2s, f2r, ns, nr, gs, gr, ws, wr, os_, or_):
    v = lax.axis_index("vec")
    g = lax.axis_index("gz")
    nxt = lax.rem(g + 1, GZ)
    prv = lax.rem(g + GZ - 1, GZ)
    half = v // 16
    ring = lax.rem(v, 16)
    other = (1 - half) * 16 + ring

    def zpeer(i):
        return lax.rem(g + i, GZ)

    def vpeer(i):
        return lax.rem(half + i // 16, 2) * 16 + lax.rem(ring + i, 16)

    def landed(src, dst, sent, received):
        every = pltpu.make_async_remote_copy(
            src, dst, sent, received, device_id=(vpeer(1), g), device_id_type=MESH)
        every.wait_send()
        every.wait_recv()

    barrier = pltpu.get_barrier_semaphore()

    def far(t):
        u = t // 2
        d = lax.rem(8 + ((u + 1) // 2) * (2 * lax.rem(u, 2) - 1), 16)
        return (1 - lax.rem(t, 2)) * 16 + d

    @pl.loop(0, NV - 1)
    def _(t):
        pl.semaphore_signal(barrier, inc=1, device_id=(vpeer(far(t)), g), device_id_type=MESH)

    @pl.loop(1, GZ)
    def _(i):
        pl.semaphore_signal(barrier, inc=1, device_id=(v, zpeer(i)), device_id_type=MESH)

    above = (other, lax.rem(g + half, GZ))
    below = (other, lax.rem(g + GZ - 1 + half, GZ))
    diagonal = (other, lax.rem(g + GZ - 1 + 2 * half, GZ))
    pl.semaphore_signal(barrier, inc=1, device_id=diagonal, device_id_type=MESH)

    load2 = pltpu.make_async_copy(shells_in, shells, lsem.at[2])
    load2.start()
    load0 = pltpu.make_async_copy(base, E.at[0:3, 2:10], lsem.at[0])
    load1 = pltpu.make_async_copy(tang, E.at[3:6, 2:10], lsem.at[1])
    load0.start()
    load1.start()
    load3 = pltpu.make_async_copy(lines_in, lines, lsem.at[3])
    load4 = pltpu.make_async_copy(dft_in, dft, lsem.at[4])
    load3.start()
    load4.start()
    load2.wait()
    load3.wait()
    load0.wait()
    load1.wait()
    sine = lines[N + 8:N + 9, :]
    laneid = lax.broadcasted_iota(jnp.int32, (1, N), 1)
    ahi, alo, bhi, blo = dft.at[0], dft.at[1], dft.at[2], dft.at[3]

    def rates(e, comps):
        bx, by, bz = E[0, e], E[1, e], E[2, e]
        tx, ty, tz = E[3, e], E[4, e], E[5, e]
        for c in comps:
            f = E[c, e]
            xp, xm, yp, ym, zp, zm = up(f, 1), down(f, 1), up(f, 0), down(f, 0), E[c, e + 1], E[c, e - 1]
            dx, dy, dz = xp - xm, yp - ym, zp - zm
            lap = ((xp + xm) + (yp + ym)) + (zp + zm) - 6.0 * f
            brate = lap * lap_scale - (bx * dx + by * dy + bz * dz) * half_inv
            if c == 0:
                zz = g * LZ + (e - 2)
                picks = jnp.zeros((1, N), f32)
                for j in range(4):
                    picks = picks + jnp.where(laneid == lax.rem(shells[j] * zz, N), sine, 0.0)
                brate = brate + jnp.sum(picks, axis=1, keepdims=True) * forcing_amplitude
            Rt[c, e - 1] = brate
            adv = tx * dx + ty * dy + tz * dz
            f = E[c + 3, e]
            xp, xm, yp, ym, zp, zm = up(f, 1), down(f, 1), up(f, 0), down(f, 0), E[c + 3, e + 1], E[c + 3, e - 1]
            lap = ((xp + xm) + (yp + ym)) + (zp + zm) - 6.0 * f
            adv = adv + (bx * (xp - xm) + by * (yp - ym) + bz * (zp - zm))
            trate = lap * lap_scale - adv * half_inv
            Rt[c + 3, e - 1] = trate
            if len(comps) == 3:
                z = e - 2
                YS[pl.ds((z // 4) * 16, 16), c, lax.rem(z, 4)] = (f + time_step * trate).reshape(16, 8, N)

    @pl.loop(0, 2)
    def _(i):
        rates(3 + 3 * i, (0, 1, 2))

    pl.semaphore_wait(barrier, GZ + NV - 1)

    halos = []
    for f, src in ((3, tang), (0, base)):
        for who, a, b in ((nxt, (LZ - 1, LZ - 2), (1, 0)), (prv, (0, 0), (10, 10))):
            n = len(halos)
            halos.append(pltpu.make_async_remote_copy(
                src.at[0:2, a[0]:a[0] + 1], E.at[f:f + 2, b[0]:b[0] + 1],
                hs.at[n], hr.at[n], device_id=(v, who), device_id_type=MESH))
            n += 1
            halos.append(pltpu.make_async_remote_copy(
                src.at[2, a[1]:a[1] + 2], E.at[f + 2, b[1]:b[1] + 2],
                hs.at[n], hr.at[n], device_id=(v, who), device_id_type=MESH))
    for h in halos:
        h.start()

    def first(i):
        p = vpeer(i)
        z = 1 - p // 16
        return pltpu.make_async_remote_copy(
            YS.at[p, :, z], R.at[v, :, z], xs, xr, device_id=(p, g), device_id_type=MESH)

    def inner(i):
        p = vpeer(i)
        z = 2 - p // 16
        return pltpu.make_async_remote_copy(
            YS.at[p, :, pl.ds(z, 2)], R.at[v, :, pl.ds(z, 2)],
            ys, yr, device_id=(p, g), device_id_type=MESH)

    def outer(i):
        p = vpeer(i)
        z = 3 * (p // 16)
        return pltpu.make_async_remote_copy(
            YS.at[p, :, z], R.at[v, :, z], es, er, device_id=(p, g), device_id_type=MESH)

    @pl.loop(1, NV)
    def _(i):
        first(i).start()

    @pl.loop(0, 4)
    def _(i):
        rates(4 + i + i // 2, (0, 1, 2))

    @pl.loop(1, NV)
    def _(i):
        inner(i).start()

    for h in halos:
        h.wait()

    @pl.loop(0, 2)
    def _(i):
        rates(2 + 7 * i, (0, 1, 2))

    @pl.loop(0, 2)
    def _(i):
        rates(1 + 9 * i, (2,))

    load4.wait()

    @pl.loop(0, LZ // 2)
    def _(p):
        parts = []
        for q in range(2):
            r = 2 * p + q + 1
            div = []
            for f in (0, 3):
                rx, ry = Rt[f, r], Rt[f + 1, r]
                d = (up(rx, 1) - down(rx, 1)) + (up(ry, 0) - down(ry, 0)) + (Rt[f + 2, r + 1] - Rt[f + 2, r - 1])
                div.append(d * half_inv)
            parts.append(right(jnp.concatenate(div, axis=1), ahi[...], alo[...]))
        rhs = jnp.concatenate([
            jnp.concatenate([parts[0][:, :N], parts[1][:, :N]], axis=1),
            jnp.concatenate([parts[0][:, N:], parts[1][:, N:]], axis=1)], axis=0)
        y = left(bhi[...], blo[...], rhs)
        for q in range(2):
            z8 = pl.multiple_of((2 * p + q) * 8, 8)
            for r in range(2):
                S[:, r, pl.ds(z8, 8), :] = y[r * N:(r + 1) * N, q * N:(q + 1) * N].reshape(GZ, 8, N)

    def a2a1(i):
        p = zpeer(i)
        return pltpu.make_async_remote_copy(
            S.at[p], T.at[:, pl.ds(pl.multiple_of(g * 64, 64), 64), :],
            a1s, a1r, device_id=(v, p), device_id_type=MESH)

    @pl.loop(1, GZ)
    def _(i):
        a2a1(i).start()

    @pl.loop(1, NV)
    def _(i):
        outer(i).start()

    keep = pltpu.make_async_copy(YS.at[v], R.at[v], lsem.at[5])
    keep.start()
    own = pltpu.make_async_copy(S.at[g], T.at[:, pl.ds(pl.multiple_of(g * 64, 64), 64), :], lsem.at[0])
    own.start()
    own.wait()

    landed(S.at[0:GZ - 1], T.at[:, 0:64 * (GZ - 1)], a1s, a1r)

    @pl.loop(0, 4)
    def _(p):
        blocks = [[T[r, pl.ds(2 * p + q, N, stride=8), :] for q in range(2)] for r in range(2)]
        rhs = jnp.concatenate([jnp.concatenate(b, axis=1) for b in blocks], axis=0)
        y = left(bhi[...], blo[...], rhs)
        kz = lax.broadcasted_iota(jnp.int32, (N, N), 0)
        kx = lax.broadcasted_iota(jnp.int32, (N, N), 1)
        qs = []
        for q in range(2):
            ky = g * 8 + 2 * p + q
            rest = (lax.rem(kz, 64) == 0) & (lax.rem(kx, 64) == 0) & (lax.rem(ky, 64) == 0)
            sq = lines[0:N, :] + (lines[N:N + 1, :] + lines[pl.ds(ky, 1), :])
            qs.append(jnp.where(rest, 0.0, (-1.0 / (N * N * N)) / jnp.where(rest, 1.0, sq)))
        qq = jnp.concatenate(qs, axis=1)
        y = jnp.concatenate([y[:N] * qq, y[N:] * qq], axis=0)
        y = left(ahi[...], alo[...], y)
        for r in range(2):
            for q in range(2):
                T2[r, pl.ds(2 * p + q, N, stride=8), :] = y[r * N:(r + 1) * N, q * N:(q + 1) * N]

    def a2a2(i):
        p = zpeer(i)
        return pltpu.make_async_remote_copy(
            T2.at[:, pl.ds(pl.multiple_of(p * 64, 64), 64), :], S2.at[g],
            a2s, a2r, device_id=(v, p), device_id_type=MESH)

    @pl.loop(1, GZ)
    def _(i):
        a2a2(i).start()

    own = pltpu.make_async_copy(T2.at[:, pl.ds(pl.multiple_of(g * 64, 64), 64), :], S2.at[g], lsem.at[1])
    own.start()
    own.wait()

    landed(T2.at[:, 0:64 * (GZ - 1)], S2.at[0:GZ - 1], a2s, a2r)

    @pl.loop(0, LZ // 2)
    def _(p):
        blocks = []
        for r in range(2):
            blocks.append(jnp.concatenate(
                [S2[:, r, pl.ds(pl.multiple_of((2 * p + q) * 8, 8), 8), :].reshape(N, N) for q in range(2)], axis=1))
        y = left(ahi[...], alo[...], jnp.concatenate(blocks, axis=0))
        for q in range(2):
            c = jnp.concatenate([y[:N, q * N:(q + 1) * N], y[N:, q * N:(q + 1) * N]], axis=1)
            phi = right(c, bhi[...], blo[...])
            z = 2 * p + q
            Pf[z + 1] = phi[:, :N]
            PS[pl.ds((z // 4) * 16, 16), (2 - lax.rem(p, 2)) if q else 3 * lax.rem(p, 2)] = phi[:, N:].reshape(16, 8, N)

    def phis(i):
        p = vpeer(i)
        return pltpu.make_async_remote_copy(
            PS.at[p, 0:2], RE.at[v, 1:3], fs, fr, device_id=(p, g), device_id_type=MESH)

    def phis2(i):
        p = vpeer(i)
        return pltpu.make_async_remote_copy(
            PS.at[p, 2:4], RE.at[v, 4:6], f2s, f2r, device_id=(p, g), device_id_type=MESH)

    @pl.loop(1, NV)
    def _(i):
        phis(i).start()

    @pl.loop(1, NV)
    def _(i):
        phis2(i).start()

    mine = pltpu.make_async_copy(PS.at[v, 0:2], RE.at[v, 1:3], lsem.at[0])
    mine.start()
    mine2 = pltpu.make_async_copy(PS.at[v, 2:4], RE.at[v, 4:6], lsem.at[6])
    mine2.start()

    y8 = pl.multiple_of((v // 2) * 8, 8)
    odd = lax.rem(v, 2) == 1
    edge0 = pltpu.make_async_remote_copy(
        Pf.at[LZ, pl.ds(y8, 8)], Pf.at[0, pl.ds(y8, 8)], ps.at[0], pr.at[0], device_id=(v, nxt), device_id_type=MESH)
    edge1 = pltpu.make_async_remote_copy(
        Pf.at[1, pl.ds(y8, 8)], Pf.at[LZ + 1, pl.ds(y8, 8)], ps.at[1], pr.at[1], device_id=(v, prv), device_id_type=MESH)
    edge0.start()
    edge1.start()

    @pl.loop(0, LZ)
    def _(z):
        phi = Pf[z + 1]
        BN[0, z] = up(phi, 1) - down(phi, 1)
        BN[1, z] = up(phi, 0) - down(phi, 0)

    edge0.wait()
    edge1.wait()

    @pl.loop(0, LZ // 2)
    def _(p):
        rows = pl.ds(y8, 8)
        for c in range(3):
            pair = []
            for q in range(2):
                z = 2 * p + q
                grad = (Pf[z + 2, rows] - Pf[z, rows]) if c == 2 else BN[c, z, rows]
                blk = E[c, z + 2, rows] + time_step * (Rt[c, z + 1, rows] - grad * half_inv)
                pair.append(jnp.where(odd, blk[4:8], blk[0:4]))
            base_out[pl.ds(pl.multiple_of(c * 4 * LZ + p * 8, 8), 8), :] = jnp.concatenate(pair, axis=0)

    mine.wait()
    keep.wait()

    landed(YS.at[0:NV - 1, :, 0], R.at[0:NV - 1, :, 0], xs, xr)

    landed(YS.at[0:NV - 1, :, 0:2], R.at[0:NV - 1, :, 0:2], ys, yr)

    landed(YS.at[0:NV - 1, :, 0], R.at[0:NV - 1, :, 0], es, er)

    landed(PS.at[0:NV - 1, 0:2], RE.at[0:NV - 1, 1:3], fs, fr)

    rimhi = half * 16 + lax.rem(ring + 1, 16)
    rimlo = half * 16 + lax.rem(ring + 15, 16)
    rims = [
        pltpu.make_async_remote_copy(hsend.at[0], hrecv.at[0], ns.at[0], nr.at[0], device_id=(rimhi, g), device_id_type=MESH),
        pltpu.make_async_remote_copy(hsend.at[1], hrecv.at[1], ns.at[1], nr.at[1], device_id=(rimlo, g), device_id_type=MESH),
        pltpu.make_async_remote_copy(RE.at[:, 2], RE.at[:, 0], ns.at[2], nr.at[2], device_id=above, device_id_type=MESH),
        pltpu.make_async_remote_copy(RE.at[:, 1], RE.at[:, 3], ns.at[3], nr.at[3], device_id=below, device_id_type=MESH),
    ]
    rims[2].start()
    rims[3].start()
    mine2.wait()

    landed(PS.at[0:NV - 1, 2:4], RE.at[0:NV - 1, 4:6], f2s, f2r)

    slot = (0, 1, 4, 5, 2, 3)
    for z in range(4):
        hsend[0, z * NV:(z + 1) * NV] = RE[:, slot[z + 1], 7, :]
        hsend[1, z * NV:(z + 1) * NV] = RE[:, slot[z + 1], 0, :]
    rims[0].start()
    rims[1].start()
    sub = lax.broadcasted_iota(jnp.int32, (8, N), 0)

    def gram_step(k, acc):
        cols = [V2[pl.ds(8 * k + j, NV, stride=ROWS), :] for j in range(8)]
        x = jnp.concatenate(cols, axis=1)
        X[k] = x
        return acc + lax.dot_general(x, x, (((1,), (1,)), ((), ())), precision=lax.Precision.HIGHEST,
                                     preferred_element_type=f32)

    def form(c, acc):
        @pl.loop(0, NV)
        def _(j):
            for z in range(4):
                phi = RE[j, slot[z + 1]]
                if c == 0:
                    grad = up(phi, 1) - down(phi, 1)
                elif c == 1:
                    rim = HB[pl.ds(pl.multiple_of((z * NV + j) * 8, 8), 8), :]
                    grad = jnp.where(sub == 7, rim, pltpu.roll(phi, 7, 0)) - jnp.where(sub == 0, rim, pltpu.roll(phi, 1, 0))
                else:
                    grad = RE[j, slot[z + 2]] - RE[j, slot[z]]
                V2[pl.ds(pl.multiple_of(j * ROWS + c * 32 + z * 8, 8), 8), :] = R[j, c, z] - (time_step * half_inv) * grad

        return lax.fori_loop(4 * c, 4 * c + 4, gram_step, acc)

    gram = form(0, jnp.zeros((NV, NV), f32))
    rims[2].wait()
    rims[3].wait()
    gram = form(2, gram)
    rims[0].wait()
    rims[1].wait()
    HB[pl.ds(0, N, stride=8), :] = hrecv[0]
    HB[pl.ds(7, N, stride=8), :] = hrecv[1]
    gram = form(1, gram)
    gbuf[...] = jnp.zeros((NV, N), f32)
    gbuf[:, 0:NV] = gram
    full = gbuf[...]
    packed = full[0:8]
    for b in range(1, 4):
        packed = packed + pltpu.roll(full[8 * b:8 * b + 8], 32 * b, 1)

    gsend[...] = packed
    grecv[g] = packed

    def ex1(i):
        return pltpu.make_async_remote_copy(
            gsend, grecv.at[g], gs, gr, device_id=(v, zpeer(i)), device_id_type=MESH)

    @pl.loop(1, GZ)
    def _(i):
        ex1(i).start()

    landed(grecv.at[0:GZ - 1], grecv.at[0:GZ - 1], gs, gr)

    total = grecv[0]
    for i in range(1, GZ):
        total = total + grecv[i]
    vsend[...] = total
    vrecv[v] = total

    def ex2(i):
        return pltpu.make_async_remote_copy(
            vsend, vrecv.at[v], ws, wr, device_id=(vpeer(i), g), device_id_type=MESH)

    @pl.loop(0, NV - 1)
    def _(t):
        ex2(far(t)).start()

    landed(vrecv.at[0:NV - 1], vrecv.at[0:NV - 1], ws, wr)

    total = vrecv[0]
    for i in range(1, NV):
        total = total + vrecv[i]
    total = total / (3.0 * N * N * N)
    lane = lax.broadcasted_iota(jnp.int32, (NV, N), 1)
    row = lax.broadcasted_iota(jnp.int32, (NV, N), 0)
    m = jnp.concatenate([total] + [pltpu.roll(total, N - 32 * b, 1) for b in range(1, 4)], axis=0)
    m = jnp.where(lane < NV, m, jnp.where(lane == row + NV, 1.0, 0.0))
    for k in range(NV - 1):
        col = jnp.broadcast_to(m[:, k:k + 1], (NV, N))
        prow = m[k:k + 1, :]
        piv = col[k:k + 1, :]
        fac = jnp.where(row > k, col * (1.0 / piv), 0.0)
        m = m - fac * prow
    diag = jnp.where(lane == row, m, 0.0)
    dcol = jnp.sum(diag, axis=1, keepdims=True)
    drow = jnp.sum(diag, axis=0, keepdims=True)
    growth[...] = (0.5 * jnp.log(drow))[0, 0:NV]
    inv = pltpu.roll(m, N - NV, 1) * (1.0 / jnp.sqrt(dcol))
    inv = inv[:, 0:NV]

    def a2a4(c, i):
        p = vpeer(i)
        return pltpu.make_async_remote_copy(
            O5.at[p, c], ortho.at[c, pl.ds(half * 4, 4), ring],
            os_, or_, device_id=(p, g), device_id_type=MESH)

    for c in range(3):
        @pl.loop(0, 4)
        def _(z):
            o = lax.dot_general(inv, X[4 * c + z], (((1,), (0,)), ((), ())), precision=lax.Precision.HIGHEST,
                                preferred_element_type=f32)
            for j in range(8):
                O5[:, c, z, j, :] = o[:, j * N:(j + 1) * N]

        @pl.loop(0, NV - 1)
        def _(t):
            a2a4(c, far(t)).start()

    own = pltpu.make_async_copy(O5.at[v], ortho.at[:, pl.ds(half * 4, 4), ring], lsem.at[1])
    own.start()
    own.wait()

    landed(O5.at[0:NV - 1], O5.at[0:NV - 1], os_, or_)


def per_device(base_flow, tangents, shells):
    dft, lines = tables()
    vm = pl.BlockSpec(memory_space=pltpu.VMEM)
    anyspace = pl.BlockSpec(memory_space=pl.ANY)
    dma = pltpu.SemaphoreType.DMA
    plane = (N, N)
    base_rows, ortho, growth = pl.pallas_call(
        kernel,
        out_shape=(
            jax.ShapeDtypeStruct((3 * LZ * N // NV, N), f32),
            jax.ShapeDtypeStruct((3, LZ, 16, 8, N), f32),
            jax.ShapeDtypeStruct((NV,), f32),
        ),
        in_specs=[anyspace] * 5,
        out_specs=(vm, anyspace, vm),
        scratch_shapes=[
            pltpu.SMEM((4,), jnp.int32),
            pltpu.VMEM((4, 2 * N, 2 * N), bf16),
            pltpu.VMEM((N + 16, N), f32),
            pltpu.VMEM((6, 12) + plane, f32),
            pltpu.VMEM((6, 10) + plane, f32),
            pltpu.VMEM((GZ, 2, 64, N), f32),
            pltpu.VMEM((2, 1024, N), f32),
            pltpu.VMEM((2, 1024, N), f32),
            pltpu.VMEM((GZ, 2, 64, N), f32),
            pltpu.VMEM((LZ + 2,) + plane, f32),
            pltpu.VMEM((NV, 3, 4, 8, N), f32),
            pltpu.VMEM((2, LZ) + plane, f32),
            pltpu.VMEM((NV, 3, 4, 8, N), f32),
            pltpu.VMEM((NV, 4, 8, N), f32),
            pltpu.VMEM((NV, 6, 8, N), f32),
            pltpu.VMEM((2,) + plane, f32),
            pltpu.VMEM((2,) + plane, f32),
            pltpu.VMEM((8 * N, N), f32),
            pltpu.VMEM((3 * LZ * N, N), f32),
            pltpu.VMEM((ROWS // 8, NV, 8 * N), f32),
            pltpu.VMEM((NV, 3, 4, 8, N), f32),
            pltpu.VMEM((NV, N), f32),
            pltpu.VMEM((8, N), f32),
            pltpu.VMEM((GZ, 8, N), f32),
            pltpu.VMEM((8, N), f32),
            pltpu.VMEM((NV, 8, N), f32),
            dma((7,)),
            dma((8,)), dma((8,)),
            dma(()), dma(()),
            dma(()), dma(()),
            dma((2,)), dma((2,)),
        ] + [dma(())] * 10 + [
            dma((4,)), dma((4,)),
        ] + [dma(())] * 6,
        compiler_params=pltpu.CompilerParams(
            collective_id=0, has_side_effects=True, vmem_limit_bytes=58 * 1024 * 1024
        ),
    )(
        shells, base_flow, tangents[0], jnp.asarray(dft), jnp.asarray(lines),
    )
    return base_rows.reshape(3, LZ, N // NV, N), ortho.reshape(tangents.shape), growth


def solution(mesh):
    in_specs = (P(None, "gz", None, None), P("vec", None, "gz", None, None), P())
    out_specs = (P(None, "gz", "vec", None), P("vec", None, "gz", None, None), P())
    return jax.shard_map(
        per_device, mesh=mesh, in_specs=in_specs, out_specs=out_specs, check_vma=False
    )
```

```python
import functools
import math

import jax
import jax.numpy as jnp
import numpy as np
from jax import lax
from jax.experimental import pallas as pl
from jax.experimental.pallas import tpu as pltpu
from jax.sharding import PartitionSpec as P

N = 128
GZ = 16
NV = 32
LZ = N // GZ
ROWS = 3 * LZ * N // NV
time_step = 0.005
viscosity = 0.01
forcing_amplitude = 4.0
spacing = 2.0 * math.pi / N
half_inv = 1.0 / (2.0 * spacing)
lap_scale = viscosity / (spacing * spacing)
f32, bf16 = jnp.float32, jnp.bfloat16
MESH = pl.DeviceIdType.MESH


def tables():
    k = np.arange(N)
    angle = 2.0 * np.pi / N * ((k[:, None] * k[None, :]) % N)
    c, s = np.cos(angle), np.sin(angle)
    a = np.block([[c, -s], [s, c]]).astype(np.float32)
    hi = a.astype(jnp.bfloat16)
    lo = (a - hi.astype(np.float32)).astype(jnp.bfloat16)
    sine = np.sin(2.0 * np.pi / N * k)
    sine[[0, 64]] = 0.0
    slope2 = ((sine / spacing) ** 2).astype(np.float32)
    lines = np.zeros((N + 16, N), np.float32)
    lines[:N] = slope2[:, None]
    lines[N] = slope2
    lines[N + 8] = sine
    return np.stack([hi, lo, hi.T, lo.T]), lines


def split(x):
    hi = x.astype(bf16)
    return hi, (x - hi.astype(f32)).astype(bf16)


def dot(a, b):
    return jnp.dot(a, b, preferred_element_type=f32)


def right(x, hi, lo):
    xh, xl = split(x)
    return dot(xh, hi) + (dot(xl, hi) + dot(xh, lo))


def left(hi, lo, x):
    xh, xl = split(x)
    return dot(hi, xh) + (dot(hi, xl) + dot(lo, xh))


def up(x, axis):
    return pltpu.roll(x, N - 1, axis)


def down(x, axis):
    return pltpu.roll(x, 1, axis)


def kernel(shells_in, base, tang, dft_in, lines_in,
           base_out, ortho, growth,
           shells, dft, lines, E, Rt, S, T, T2, S2, Pf, YS, BN, R, PS, RE, hsend, hrecv, HB, V2, X, O5, gbuf, gsend, grecv, vsend, vrecv,
           lsem, hs, hr, a1s, a1r, a2s, a2r, ps, pr, xs, xr, ys, yr, es, er, fs, fr, f2s, f2r, ns, nr, gs, gr, ws, wr, os_, or_):
    v = lax.axis_index("vec")
    g = lax.axis_index("gz")
    nxt = lax.rem(g + 1, GZ)
    prv = lax.rem(g + GZ - 1, GZ)
    half = v // 16
    ring = lax.rem(v, 16)
    other = (1 - half) * 16 + ring

    def zpeer(i):
        return lax.rem(g + i, GZ)

    def vpeer(i):
        return lax.rem(half + i // 16, 2) * 16 + lax.rem(ring + i, 16)

    def landed(src, dst, sent, received):
        every = pltpu.make_async_remote_copy(
            src, dst, sent, received, device_id=(vpeer(1), g), device_id_type=MESH)
        every.wait_send()
        every.wait_recv()

    barrier = pltpu.get_barrier_semaphore()

    def far(t):
        u = t // 2
        d = lax.rem(8 + ((u + 1) // 2) * (2 * lax.rem(u, 2) - 1), 16)
        return (1 - lax.rem(t, 2)) * 16 + d

    @pl.loop(0, NV - 1)
    def _(t):
        pl.semaphore_signal(barrier, inc=1, device_id=(vpeer(far(t)), g), device_id_type=MESH)

    @pl.loop(1, GZ)
    def _(i):
        pl.semaphore_signal(barrier, inc=1, device_id=(v, zpeer(i)), device_id_type=MESH)

    above = (other, lax.rem(g + half, GZ))
    below = (other, lax.rem(g + GZ - 1 + half, GZ))
    diagonal = (other, lax.rem(g + GZ - 1 + 2 * half, GZ))
    pl.semaphore_signal(barrier, inc=1, device_id=diagonal, device_id_type=MESH)

    load2 = pltpu.make_async_copy(shells_in, shells, lsem.at[2])
    load2.start()
    load0 = pltpu.make_async_copy(base, E.at[0:3, 2:10], lsem.at[0])
    load1 = pltpu.make_async_copy(tang, E.at[3:6, 2:10], lsem.at[1])
    load0.start()
    load1.start()
    load3 = pltpu.make_async_copy(lines_in, lines, lsem.at[3])
    load4 = pltpu.make_async_copy(dft_in, dft, lsem.at[4])
    load3.start()
    load4.start()
    load2.wait()
    load3.wait()
    load0.wait()
    load1.wait()
    sine = lines[N + 8:N + 9, :]
    laneid = lax.broadcasted_iota(jnp.int32, (1, N), 1)
    ahi, alo, bhi, blo = dft.at[0], dft.at[1], dft.at[2], dft.at[3]

    def rates(e, comps):
        bx, by, bz = E[0, e], E[1, e], E[2, e]
        tx, ty, tz = E[3, e], E[4, e], E[5, e]
        for c in comps:
            f = E[c, e]
            xp, xm, yp, ym, zp, zm = up(f, 1), down(f, 1), up(f, 0), down(f, 0), E[c, e + 1], E[c, e - 1]
            dx, dy, dz = xp - xm, yp - ym, zp - zm
            lap = ((xp + xm) + (yp + ym)) + (zp + zm) - 6.0 * f
            brate = lap * lap_scale - (bx * dx + by * dy + bz * dz) * half_inv
            if c == 0:
                zz = g * LZ + (e - 2)
                picks = jnp.zeros((1, N), f32)
                for j in range(4):
                    picks = picks + jnp.where(laneid == lax.rem(shells[j] * zz, N), sine, 0.0)
                brate = brate + jnp.sum(picks, axis=1, keepdims=True) * forcing_amplitude
            Rt[c, e - 1] = brate
            adv = tx * dx + ty * dy + tz * dz
            f = E[c + 3, e]
            xp, xm, yp, ym, zp, zm = up(f, 1), down(f, 1), up(f, 0), down(f, 0), E[c + 3, e + 1], E[c + 3, e - 1]
            lap = ((xp + xm) + (yp + ym)) + (zp + zm) - 6.0 * f
            adv = adv + (bx * (xp - xm) + by * (yp - ym) + bz * (zp - zm))
            trate = lap * lap_scale - adv * half_inv
            Rt[c + 3, e - 1] = trate
            if len(comps) == 3:
                z = e - 2
                YS[pl.ds((z // 4) * 16, 16), c, lax.rem(z, 4)] = (f + time_step * trate).reshape(16, 8, N)

    @pl.loop(0, 2)
    def _(i):
        rates(3 + 3 * i, (0, 1, 2))

    pl.semaphore_wait(barrier, GZ + NV - 1)

    halos = []
    for f, src in ((3, tang), (0, base)):
        for who, a, b in ((nxt, (LZ - 1, LZ - 2), (1, 0)), (prv, (0, 0), (10, 10))):
            n = len(halos)
            halos.append(pltpu.make_async_remote_copy(
                src.at[0:2, a[0]:a[0] + 1], E.at[f:f + 2, b[0]:b[0] + 1],
                hs.at[n], hr.at[n], device_id=(v, who), device_id_type=MESH))
            n += 1
            halos.append(pltpu.make_async_remote_copy(
                src.at[2, a[1]:a[1] + 2], E.at[f + 2, b[1]:b[1] + 2],
                hs.at[n], hr.at[n], device_id=(v, who), device_id_type=MESH))
    for h in halos:
        h.start()

    def first(i):
        p = vpeer(i)
        z = 1 - p // 16
        return pltpu.make_async_remote_copy(
            YS.at[p, :, z], R.at[v, :, z], xs, xr, device_id=(p, g), device_id_type=MESH)

    def inner(i):
        p = vpeer(i)
        z = 2 - p // 16
        return pltpu.make_async_remote_copy(
            YS.at[p, :, pl.ds(z, 2)], R.at[v, :, pl.ds(z, 2)],
            ys, yr, device_id=(p, g), device_id_type=MESH)

    def outer(i):
        p = vpeer(i)
        z = 3 * (p // 16)
        return pltpu.make_async_remote_copy(
            YS.at[p, :, z], R.at[v, :, z], es, er, device_id=(p, g), device_id_type=MESH)

    @pl.loop(1, NV)
    def _(i):
        first(i).start()

    @pl.loop(0, 4)
    def _(i):
        rates(4 + i + i // 2, (0, 1, 2))

    @pl.loop(1, NV)
    def _(i):
        inner(i).start()

    for h in halos:
        h.wait()

    @pl.loop(0, 2)
    def _(i):
        rates(2 + 7 * i, (0, 1, 2))

    @pl.loop(0, 2)
    def _(i):
        rates(1 + 9 * i, (2,))

    load4.wait()

    @pl.loop(0, LZ // 2)
    def _(p):
        parts = []
        for q in range(2):
            r = 2 * p + q + 1
            div = []
            for f in (0, 3):
                rx, ry = Rt[f, r], Rt[f + 1, r]
                d = (up(rx, 1) - down(rx, 1)) + (up(ry, 0) - down(ry, 0)) + (Rt[f + 2, r + 1] - Rt[f + 2, r - 1])
                div.append(d * half_inv)
            parts.append(right(jnp.concatenate(div, axis=1), ahi[...], alo[...]))
        rhs = jnp.concatenate([
            jnp.concatenate([parts[0][:, :N], parts[1][:, :N]], axis=1),
            jnp.concatenate([parts[0][:, N:], parts[1][:, N:]], axis=1)], axis=0)
        y = left(bhi[...], blo[...], rhs)
        for q in range(2):
            z8 = pl.multiple_of((2 * p + q) * 8, 8)
            for r in range(2):
                S[:, r, pl.ds(z8, 8), :] = y[r * N:(r + 1) * N, q * N:(q + 1) * N].reshape(GZ, 8, N)

    def a2a1(i):
        p = zpeer(i)
        return pltpu.make_async_remote_copy(
            S.at[p], T.at[:, pl.ds(pl.multiple_of(g * 64, 64), 64), :],
            a1s, a1r, device_id=(v, p), device_id_type=MESH)

    @pl.loop(1, GZ)
    def _(i):
        a2a1(i).start()

    @pl.loop(1, NV)
    def _(i):
        outer(i).start()

    keep = pltpu.make_async_copy(YS.at[v], R.at[v], lsem.at[5])
    keep.start()
    own = pltpu.make_async_copy(S.at[g], T.at[:, pl.ds(pl.multiple_of(g * 64, 64), 64), :], lsem.at[0])
    own.start()
    own.wait()

    landed(S.at[0:GZ - 1], T.at[:, 0:64 * (GZ - 1)], a1s, a1r)

    @pl.loop(0, 4)
    def _(p):
        blocks = [[T[r, pl.ds(2 * p + q, N, stride=8), :] for q in range(2)] for r in range(2)]
        rhs = jnp.concatenate([jnp.concatenate(b, axis=1) for b in blocks], axis=0)
        y = left(bhi[...], blo[...], rhs)
        kz = lax.broadcasted_iota(jnp.int32, (N, N), 0)
        kx = lax.broadcasted_iota(jnp.int32, (N, N), 1)
        qs = []
        for q in range(2):
            ky = g * 8 + 2 * p + q
            rest = (lax.rem(kz, 64) == 0) & (lax.rem(kx, 64) == 0) & (lax.rem(ky, 64) == 0)
            sq = lines[0:N, :] + (lines[N:N + 1, :] + lines[pl.ds(ky, 1), :])
            qs.append(jnp.where(rest, 0.0, (-1.0 / (N * N * N)) / jnp.where(rest, 1.0, sq)))
        qq = jnp.concatenate(qs, axis=1)
        y = jnp.concatenate([y[:N] * qq, y[N:] * qq], axis=0)
        y = left(ahi[...], alo[...], y)
        for r in range(2):
            for q in range(2):
                T2[r, pl.ds(2 * p + q, N, stride=8), :] = y[r * N:(r + 1) * N, q * N:(q + 1) * N]

    def a2a2(i):
        p = zpeer(i)
        return pltpu.make_async_remote_copy(
            T2.at[:, pl.ds(pl.multiple_of(p * 64, 64), 64), :], S2.at[g],
            a2s, a2r, device_id=(v, p), device_id_type=MESH)

    @pl.loop(1, GZ)
    def _(i):
        a2a2(i).start()

    own = pltpu.make_async_copy(T2.at[:, pl.ds(pl.multiple_of(g * 64, 64), 64), :], S2.at[g], lsem.at[1])
    own.start()
    own.wait()

    landed(T2.at[:, 0:64 * (GZ - 1)], S2.at[0:GZ - 1], a2s, a2r)

    @pl.loop(0, LZ // 2)
    def _(p):
        blocks = []
        for r in range(2):
            blocks.append(jnp.concatenate(
                [S2[:, r, pl.ds(pl.multiple_of((2 * p + q) * 8, 8), 8), :].reshape(N, N) for q in range(2)], axis=1))
        y = left(ahi[...], alo[...], jnp.concatenate(blocks, axis=0))
        for q in range(2):
            c = jnp.concatenate([y[:N, q * N:(q + 1) * N], y[N:, q * N:(q + 1) * N]], axis=1)
            phi = right(c, bhi[...], blo[...])
            z = 2 * p + q
            Pf[z + 1] = phi[:, :N]
            PS[pl.ds((z // 4) * 16, 16), (2 - lax.rem(p, 2)) if q else 3 * lax.rem(p, 2)] = phi[:, N:].reshape(16, 8, N)

    def phis(i):
        p = vpeer(i)
        return pltpu.make_async_remote_copy(
            PS.at[p, 0:2], RE.at[v, 1:3], fs, fr, device_id=(p, g), device_id_type=MESH)

    def phis2(i):
        p = vpeer(i)
        return pltpu.make_async_remote_copy(
            PS.at[p, 2:4], RE.at[v, 4:6], f2s, f2r, device_id=(p, g), device_id_type=MESH)

    @pl.loop(1, NV)
    def _(i):
        phis(i).start()

    @pl.loop(1, NV)
    def _(i):
        phis2(i).start()

    mine = pltpu.make_async_copy(PS.at[v, 0:2], RE.at[v, 1:3], lsem.at[0])
    mine.start()
    mine2 = pltpu.make_async_copy(PS.at[v, 2:4], RE.at[v, 4:6], lsem.at[6])
    mine2.start()

    y8 = pl.multiple_of((v // 2) * 8, 8)
    odd = lax.rem(v, 2) == 1
    edge0 = pltpu.make_async_remote_copy(
        Pf.at[LZ, pl.ds(y8, 8)], Pf.at[0, pl.ds(y8, 8)], ps.at[0], pr.at[0], device_id=(v, nxt), device_id_type=MESH)
    edge1 = pltpu.make_async_remote_copy(
        Pf.at[1, pl.ds(y8, 8)], Pf.at[LZ + 1, pl.ds(y8, 8)], ps.at[1], pr.at[1], device_id=(v, prv), device_id_type=MESH)
    edge0.start()
    edge1.start()

    @pl.loop(0, LZ)
    def _(z):
        phi = Pf[z + 1]
        BN[0, z] = up(phi, 1) - down(phi, 1)
        BN[1, z] = up(phi, 0) - down(phi, 0)

    edge0.wait()
    edge1.wait()

    @pl.loop(0, LZ // 2)
    def _(p):
        rows = pl.ds(y8, 8)
        for c in range(3):
            pair = []
            for q in range(2):
                z = 2 * p + q
                grad = (Pf[z + 2, rows] - Pf[z, rows]) if c == 2 else BN[c, z, rows]
                blk = E[c, z + 2, rows] + time_step * (Rt[c, z + 1, rows] - grad * half_inv)
                pair.append(jnp.where(odd, blk[4:8], blk[0:4]))
            base_out[pl.ds(pl.multiple_of(c * 4 * LZ + p * 8, 8), 8), :] = jnp.concatenate(pair, axis=0)

    mine.wait()
    keep.wait()

    landed(YS.at[0:NV - 1, :, 0], R.at[0:NV - 1, :, 0], xs, xr)

    landed(YS.at[0:NV - 1, :, 0:2], R.at[0:NV - 1, :, 0:2], ys, yr)

    landed(YS.at[0:NV - 1, :, 0], R.at[0:NV - 1, :, 0], es, er)

    landed(PS.at[0:NV - 1, 0:2], RE.at[0:NV - 1, 1:3], fs, fr)

    rimhi = half * 16 + lax.rem(ring + 1, 16)
    rimlo = half * 16 + lax.rem(ring + 15, 16)
    rims = [
        pltpu.make_async_remote_copy(hsend.at[0], hrecv.at[0], ns.at[0], nr.at[0], device_id=(rimhi, g), device_id_type=MESH),
        pltpu.make_async_remote_copy(hsend.at[1], hrecv.at[1], ns.at[1], nr.at[1], device_id=(rimlo, g), device_id_type=MESH),
        pltpu.make_async_remote_copy(RE.at[:, 2], RE.at[:, 0], ns.at[2], nr.at[2], device_id=above, device_id_type=MESH),
        pltpu.make_async_remote_copy(RE.at[:, 1], RE.at[:, 3], ns.at[3], nr.at[3], device_id=below, device_id_type=MESH),
    ]
    rims[2].start()
    rims[3].start()
    mine2.wait()

    landed(PS.at[0:NV - 1, 2:4], RE.at[0:NV - 1, 4:6], f2s, f2r)

    slot = (0, 1, 4, 5, 2, 3)
    for z in range(4):
        hsend[0, z * NV:(z + 1) * NV] = RE[:, slot[z + 1], 7, :]
        hsend[1, z * NV:(z + 1) * NV] = RE[:, slot[z + 1], 0, :]
    rims[0].start()
    rims[1].start()
    sub = lax.broadcasted_iota(jnp.int32, (8, N), 0)

    def gram_step(k, acc):
        cols = [V2[pl.ds(8 * k + j, NV, stride=ROWS), :] for j in range(8)]
        x = jnp.concatenate(cols, axis=1)
        X[k] = x
        return acc + lax.dot_general(x, x, (((1,), (1,)), ((), ())), precision=lax.Precision.HIGHEST,
                                     preferred_element_type=f32)

    def form(c, acc):
        @pl.loop(0, NV)
        def _(j):
            for z in range(4):
                phi = RE[j, slot[z + 1]]
                if c == 0:
                    grad = up(phi, 1) - down(phi, 1)
                elif c == 1:
                    rim = HB[pl.ds(pl.multiple_of((z * NV + j) * 8, 8), 8), :]
                    grad = jnp.where(sub == 7, rim, pltpu.roll(phi, 7, 0)) - jnp.where(sub == 0, rim, pltpu.roll(phi, 1, 0))
                else:
                    grad = RE[j, slot[z + 2]] - RE[j, slot[z]]
                V2[pl.ds(pl.multiple_of(j * ROWS + c * 32 + z * 8, 8), 8), :] = R[j, c, z] - (time_step * half_inv) * grad

        return lax.fori_loop(4 * c, 4 * c + 4, gram_step, acc)

    gram = form(0, jnp.zeros((NV, NV), f32))
    rims[2].wait()
    rims[3].wait()
    gram = form(2, gram)
    rims[0].wait()
    rims[1].wait()
    HB[pl.ds(0, N, stride=8), :] = hrecv[0]
    HB[pl.ds(7, N, stride=8), :] = hrecv[1]
    gram = form(1, gram)
    gbuf[...] = jnp.zeros((NV, N), f32)
    gbuf[:, 0:NV] = gram
    full = gbuf[...]
    packed = full[0:8]
    for b in range(1, 4):
        packed = packed + pltpu.roll(full[8 * b:8 * b + 8], 32 * b, 1)

    gsend[...] = packed
    grecv[g] = packed

    def ex1(i):
        return pltpu.make_async_remote_copy(
            gsend, grecv.at[g], gs, gr, device_id=(v, zpeer(i)), device_id_type=MESH)

    @pl.loop(1, GZ)
    def _(i):
        ex1(i).start()

    landed(grecv.at[0:GZ - 1], grecv.at[0:GZ - 1], gs, gr)

    total = grecv[0]
    for i in range(1, GZ):
        total = total + grecv[i]
    vsend[...] = total
    vrecv[v] = total

    def ex2(i):
        return pltpu.make_async_remote_copy(
            vsend, vrecv.at[v], ws, wr, device_id=(vpeer(i), g), device_id_type=MESH)

    @pl.loop(0, NV - 1)
    def _(t):
        ex2(far(t)).start()

    landed(vrecv.at[0:NV - 1], vrecv.at[0:NV - 1], ws, wr)

    total = vrecv[0]
    for i in range(1, NV):
        total = total + vrecv[i]
    total = total / (3.0 * N * N * N)
    lane = lax.broadcasted_iota(jnp.int32, (NV, N), 1)
    row = lax.broadcasted_iota(jnp.int32, (NV, N), 0)
    m = jnp.concatenate([total] + [pltpu.roll(total, N - 32 * b, 1) for b in range(1, 4)], axis=0)
    m = jnp.where(lane < NV, m, jnp.where(lane == row + NV, 1.0, 0.0))
    for k in range(NV - 1):
        col = jnp.broadcast_to(m[:, k:k + 1], (NV, N))
        prow = m[k:k + 1, :]
        piv = col[k:k + 1, :]
        fac = jnp.where(row > k, col * (1.0 / piv), 0.0)
        m = m - fac * prow
    diag = jnp.where(lane == row, m, 0.0)
    dcol = jnp.sum(diag, axis=1, keepdims=True)
    drow = jnp.sum(diag, axis=0, keepdims=True)
    growth[...] = (0.5 * jnp.log(drow))[0, 0:NV]
    inv = pltpu.roll(m, N - NV, 1) * (1.0 / jnp.sqrt(dcol))
    inv = inv[:, 0:NV]

    def a2a4(c, i):
        p = vpeer(i)
        return pltpu.make_async_remote_copy(
            O5.at[p, c], ortho.at[c, pl.ds(half * 4, 4), ring],
            os_, or_, device_id=(p, g), device_id_type=MESH)

    for c in range(3):
        @pl.loop(0, 4)
        def _(z):
            o = lax.dot_general(inv, X[4 * c + z], (((1,), (0,)), ((), ())), precision=lax.Precision.HIGHEST,
                                preferred_element_type=f32)
            for j in range(8):
                O5[:, c, z, j, :] = o[:, j * N:(j + 1) * N]

        @pl.loop(0, NV - 1)
        def _(t):
            a2a4(c, far(t)).start()

    own = pltpu.make_async_copy(O5.at[v], ortho.at[:, pl.ds(half * 4, 4), ring], lsem.at[1])
    own.start()
    own.wait()

    landed(O5.at[0:NV - 1], O5.at[0:NV - 1], os_, or_)


def per_device(base_flow, tangents, shells):
    dft, lines = tables()
    vm = pl.BlockSpec(memory_space=pltpu.VMEM)
    anyspace = pl.BlockSpec(memory_space=pl.ANY)
    dma = pltpu.SemaphoreType.DMA
    plane = (N, N)
    base_rows, ortho, growth = pl.pallas_call(
        kernel,
        out_shape=(
            pltpu.VMEM((3 * LZ * N // NV, N), f32),
            pltpu.VMEM((3, LZ, 16, 8, N), f32),
            pltpu.VMEM((NV,), f32),
        ),
        in_specs=[anyspace] * 5,
        out_specs=(vm, vm, vm),
        scratch_shapes=[
            pltpu.SMEM((4,), jnp.int32),
            pltpu.VMEM((4, 2 * N, 2 * N), bf16),
            pltpu.VMEM((N + 16, N), f32),
            pltpu.VMEM((6, 12) + plane, f32),
            pltpu.VMEM((6, 10) + plane, f32),
            pltpu.VMEM((GZ, 2, 64, N), f32),
            pltpu.VMEM((2, 1024, N), f32),
            pltpu.VMEM((2, 1024, N), f32),
            pltpu.VMEM((GZ, 2, 64, N), f32),
            pltpu.VMEM((LZ + 2,) + plane, f32),
            pltpu.VMEM((NV, 3, 4, 8, N), f32),
            pltpu.VMEM((2, LZ) + plane, f32),
            pltpu.VMEM((NV, 3, 4, 8, N), f32),
            pltpu.VMEM((NV, 4, 8, N), f32),
            pltpu.VMEM((NV, 6, 8, N), f32),
            pltpu.VMEM((2,) + plane, f32),
            pltpu.VMEM((2,) + plane, f32),
            pltpu.VMEM((8 * N, N), f32),
            pltpu.VMEM((3 * LZ * N, N), f32),
            pltpu.VMEM((ROWS // 8, NV, 8 * N), f32),
            pltpu.VMEM((NV, 3, 4, 8, N), f32),
            pltpu.VMEM((NV, N), f32),
            pltpu.VMEM((8, N), f32),
            pltpu.VMEM((GZ, 8, N), f32),
            pltpu.VMEM((8, N), f32),
            pltpu.VMEM((NV, 8, N), f32),
            dma((7,)),
            dma((8,)), dma((8,)),
            dma(()), dma(()),
            dma(()), dma(()),
            dma((2,)), dma((2,)),
        ] + [dma(())] * 10 + [
            dma((4,)), dma((4,)),
        ] + [dma(())] * 6,
        compiler_params=pltpu.CompilerParams(
            collective_id=0, has_side_effects=True, vmem_limit_bytes=58 * 1024 * 1024
        ),
    )(
        shells, base_flow, tangents[0], jnp.asarray(dft), jnp.asarray(lines),
    )
    return base_rows.reshape(3, LZ, N // NV, N), ortho.reshape(tangents.shape), growth


def solution(mesh):
    in_specs = (P(None, "gz", None, None), P("vec", None, "gz", None, None), P())
    out_specs = (P(None, "gz", "vec", None), P("vec", None, "gz", None, None), P())
    return jax.shard_map(
        per_device, mesh=mesh, in_specs=in_specs, out_specs=out_specs, check_vma=False
    )
```
